256 devices in a mesh: dp: 2 (over x_lo), expert: 8 (over z), shard: 16 (over x_hi, y, core).
Axes of the slice: x: 4 (x_hi: 2, x_lo: 2; x = x_hi * 2 + x_lo), y: 4, z: 8, core: 2. Of those that a mesh axis runs over, the one named last changes fastest.
Arguments:
- tokens: bfloat16 [2048, 6144], P(('dp', 'expert', 'shard')), may hold values from -6 to 6
- gate_up_weight: bfloat16 [8, 2, 8192, 6144], P(None, None, ('dp', 'expert', 'shard')), may hold values from -0.078125 to 0.078125
- down_weight: bfloat16 [8, 8192, 6144], P(None, ('dp', 'expert', 'shard')), may hold values from -0.0625 to 0.0625
- expert_ids: int32 [2048, 2], P(('dp', 'expert', 'shard')), may hold values from 0 to 7, as said below
- slot_ids: int32 [2048, 2], P(('dp', 'expert', 'shard')), may hold values from 0 to 3, as said below
- gate_values: float32 [2048, 2], P(('dp', 'expert', 'shard')), may hold values from 0.1 to 1
- old_place: int32 [8], replicated, may hold values from 0 to 7, each once
- new_place: int32 [8], replicated, may hold values from 0 to 7, each once
Outputs:
- mixed_out: bfloat16 [2048, 6144], P(('dp', 'expert', 'shard'))
The draws below stay inside these ranges and needn't reach their ends.
Inputs may be any that keep to these rules, and one draw needn't show every extreme that they name: `expert_ids`: each token names 2 different experts; among the 8 tokens of one block no expert is named more than 4 times, and one expert is named exactly 4 times in every block. `slot_ids`: within one block, two choices that name the same expert have different slots. `old_place`: each expert number appears once. `new_place`: each expert number appears once.
All inputs are finite; a program needn't handle non-finite values.
Results may differ from the reference program's by a relative error of at most 0.02.
Values may be sent and summed in bfloat16 or wider, within the bound.
A program may use at most 128 MiB of HBM per device.

```python
import jax
import jax.numpy as jnp
from jax import lax

D = 6144
FF = 8192
TOP = 2
TOK_DEV = 8
EXPERTS = 8
BLOCKS = 256
TOKENS = 2048
CAP = 4
CLASSES = 16


def routing_table(key):
    base_key = jax.random.fold_in(key, 7177)
    favour = jax.random.randint(jax.random.fold_in(base_key, 1), (), 0, EXPERTS).astype(jnp.int32)

    def one_block(block_index):
        block_key = jax.random.fold_in(base_key, block_index + 2)
        key_rank, key_cells, key_offset, key_order, key_flip = jax.random.split(block_key, 5)
        others = jax.random.permutation(key_rank, EXPERTS - 1).astype(jnp.int32) + 1
        run_ranks = jnp.concatenate([jnp.zeros((1,), jnp.int32), others])
        run_expert = (favour + run_ranks) % EXPERTS
        cell_pick = jax.random.permutation(key_cells, (EXPERTS - 1) * CAP).astype(jnp.int32)[:2 * TOK_DEV - CAP]
        chosen = cell_pick // CAP + 1
        run_numbers = jnp.arange(EXPERTS, dtype=jnp.int32)
        counts = jnp.sum((chosen[None, :] == run_numbers[:, None]).astype(jnp.int32), axis=1)
        counts = jnp.where(run_numbers == 0, CAP, counts).astype(jnp.int32)
        run_ends = jnp.cumsum(counts).astype(jnp.int32)
        starts = run_ends - counts
        entries = jnp.arange(2 * TOK_DEV, dtype=jnp.int32)
        run_of = jnp.sum((entries[:, None] >= run_ends[None, :]).astype(jnp.int32), axis=1)
        in_run = entries - starts[run_of]
        expert = run_expert[run_of]
        offset = jax.random.randint(key_offset, (EXPERTS,), 0, CAP).astype(jnp.int32)
        slot_of = (in_run + offset[expert]) % CAP
        pair_expert = jnp.stack([expert[:TOK_DEV], expert[TOK_DEV:]], axis=1)
        pair_slot = jnp.stack([slot_of[:TOK_DEV], slot_of[TOK_DEV:]], axis=1)
        shuffle = jax.random.permutation(key_order, TOK_DEV)
        pair_expert = pair_expert[shuffle]
        pair_slot = pair_slot[shuffle]
        flipped = jax.random.randint(key_flip, (TOK_DEV, 1), 0, 2)
        pair_expert = jnp.where(flipped == 1, pair_expert[:, ::-1], pair_expert)
        pair_slot = jnp.where(flipped == 1, pair_slot[:, ::-1], pair_slot)
        return (pair_expert, pair_slot)
    experts_all, slots_all = jax.vmap(one_block)(jnp.arange(TOKENS // TOK_DEV, dtype=jnp.int32))
    return (experts_all.reshape(TOKENS, TOP).astype(jnp.int32), slots_all.reshape(TOKENS, TOP).astype(jnp.int32))


def draw_expert_ids(key, part):
    return routing_table(key)[0]


def draw_slot_ids(key, part):
    return routing_table(key)[1]


def block_levels(key, extent, cuts, low, top_value):
    level = 1.0
    for dim, shards_of in cuts:
        heights = jax.random.uniform(jax.random.fold_in(jax.random.fold_in(key, 6), dim), (shards_of,), jnp.float32, low / len(cuts), top_value / len(cuts))
        level = level * jnp.repeat(jnp.exp(heights), extent[dim] // shards_of).reshape((-1,) + (1,) * (len(extent) - 1 - dim))
    return level


def centred(stream_key, dims, spread, limit, pieces=(), kind=jnp.bfloat16):
    values = spread * jax.random.normal(stream_key, dims, jnp.float32)
    if pieces:
        values = values * block_levels(stream_key, dims, pieces, -0.22, 0.18)
    return jnp.clip(values, -limit, limit).astype(kind)


def setup_inputs(seed: int = 0) -> dict:
    key_list = jax.random.split(jax.random.key(seed), 9)
    tokens = centred(key_list[0], (TOKENS, D), 1.0, 6.0, ((0, 256),))
    gate_up_weight = centred(key_list[1], (EXPERTS, 2, FF, D), D ** -0.5, 0.078125, ((2, 256),))
    down_weight = centred(key_list[2], (EXPERTS, FF, D), FF ** -0.5, 0.0625, ((1, 256),))
    expert_ids = draw_expert_ids(jax.random.fold_in(key_list[8], 71), 0)
    slot_ids = draw_slot_ids(jax.random.fold_in(key_list[8], 71), 0)
    gate_values = jnp.clip(0.1 + 0.9 * jax.random.uniform(key_list[5], (TOKENS, TOP), jnp.float32) ** block_levels(key_list[5], (TOKENS, TOP), ((0, 256),), -0.2, 0.2), 0.1, 1.0)
    old_place = jax.random.permutation(key_list[6], EXPERTS).astype(jnp.int32)
    new_place = jax.random.permutation(key_list[7], EXPERTS).astype(jnp.int32)
    return {"tokens": tokens, "gate_up_weight": gate_up_weight, "down_weight": down_weight, "expert_ids": expert_ids, "slot_ids": slot_ids, "gate_values": gate_values, "old_place": old_place, "new_place": new_place}


def reference(tokens, gate_up_weight, down_weight, expert_ids, slot_ids, gate_values, old_place, new_place):
    cell_count = EXPERTS * CAP
    matches = (new_place[:, None] == old_place[None, :]).astype(jnp.int32)
    slot_order = jnp.sum(matches * jnp.arange(EXPERTS, dtype=jnp.int32)[None, :], axis=1).astype(jnp.int32)
    ordered_in = jnp.take(gate_up_weight, slot_order, axis=0)
    ordered_down = jnp.take(down_weight, slot_order, axis=0)
    cell_ids = (expert_ids * CAP + slot_ids).reshape(BLOCKS, TOK_DEV, TOP)
    cell_range = jnp.arange(cell_count, dtype=jnp.int32)
    cell_hits = (cell_ids[:, :, :, None] == cell_range[None, None, None, :]).astype(jnp.float32)
    token_picks = jnp.sum(cell_hits, axis=2)
    token_blocks = tokens.reshape(BLOCKS, TOK_DEV, D).astype(jnp.float32)
    dispatched = jnp.einsum("btc,btd->bcd", token_picks, token_blocks, precision=lax.Precision.HIGHEST).astype(jnp.bfloat16)
    per_expert = dispatched.reshape(BLOCKS, EXPERTS, CAP, D).transpose(1, 0, 2, 3).reshape(EXPERTS, BLOCKS * CAP, D)
    sliver = FF // BLOCKS
    groups = FF // (CLASSES * sliver)

    def one_expert(operands):
        expert_rows, pair_in, down_rows = operands
        gate_part = jnp.dot(expert_rows, pair_in[0].T, preferred_element_type=jnp.float32)
        up_part = jnp.dot(expert_rows, pair_in[1].T, preferred_element_type=jnp.float32)
        hidden = (jax.nn.silu(gate_part) * up_part).astype(jnp.bfloat16)
        row_total = expert_rows.shape[0]
        hidden_classes = hidden.reshape(row_total, groups, CLASSES, sliver)
        down_classes = down_rows.reshape(groups, CLASSES, sliver, D)

        def add_class(total, class_index):
            piece = lax.dynamic_index_in_dim(hidden_classes, class_index, 2, keepdims=False).reshape(row_total, groups * sliver)
            weight_piece = lax.dynamic_index_in_dim(down_classes, class_index, 1, keepdims=False).reshape(groups * sliver, D)
            partial_value = jnp.dot(piece, weight_piece, preferred_element_type=jnp.float32).astype(jnp.bfloat16)
            partial_value = lax.optimization_barrier(partial_value)
            return total + partial_value.astype(jnp.float32), class_index

        total, unused_index = lax.scan(add_class, jnp.zeros((row_total, D), jnp.float32), jnp.arange(CLASSES, dtype=jnp.int32))
        return total.astype(jnp.bfloat16)

    expert_out = lax.map(one_expert, (per_expert, ordered_in, ordered_down))
    returned = expert_out.reshape(EXPERTS, BLOCKS, CAP, D).transpose(1, 0, 2, 3).reshape(BLOCKS, cell_count, D)
    combine_weights = jnp.sum(cell_hits * gate_values.reshape(BLOCKS, TOK_DEV, TOP)[:, :, :, None], axis=2)
    mixed_out = jnp.einsum("btc,bcd->btd", combine_weights, returned.astype(jnp.float32), precision=lax.Precision.HIGHEST)
    return mixed_out.reshape(TOKENS, D).astype(jnp.bfloat16)
```

```python
import functools
import heapq

import jax
import jax.numpy as jnp
from jax import lax
from jax.experimental import pallas as pl
from jax.experimental.pallas import tpu as pltpu
from jax.sharding import PartitionSpec as P

AXES = ("dp", "expert", "shard")
ROWS = 8
WIDE = 2048
EXTRA = 128
SLOTS = 8
SLIVER = 32
UNITS = 2 * SLOTS * SLIVER
RING = {"x": 4, "y": 4, "z": 8}
ORDER = (("x", "y", "z"), ("z", "y", "x"), ("z", "x", "y"))
RATE, LATENCY = 44500.0, 1.8


class Message:
    def __init__(self, part, stage, dist, sign, sub):
        self.part, self.stage, self.dist, self.sign, self.sub = part, stage, dist, sign, sub
        self.key = (part, stage, dist, sign, sub)
        self.axis = ORDER[part][stage]
        self.link = (self.axis, sign)


def subs_of(part, stage):
    n1, n2 = RING[ORDER[part][0]], RING[ORDER[part][1]]
    if stage == 0:
        return [(0, 0, 1)]
    if stage == 1:
        return [(0, 0, n1 // 2), (0, n1 // 2, n1 // 2)]
    return [(i2, i1, 4) for i2 in range(n2) for i1 in range(0, n1, 4)]


def messages():
    out = []
    for part in range(3):
        for stage in range(3):
            size = RING[ORDER[part][stage]]
            subs = subs_of(part, stage)
            for dist in range(1, size // 2 + 1):
                for sign in (1, -1):
                    for sub in range(len(subs)):
                        if dist == size // 2:
                            if len(subs) == 1:
                                if sign != (-1 if part == 2 else 1):
                                    continue
                            elif (sub < len(subs) // 2) != (sign == 1):
                                continue
                        out.append(Message(part, stage, dist, sign, sub))
    return out


def blocks_of(msg, ring_index):
    i2, i1, n = subs_of(msg.part, msg.stage)[msg.sub]
    size = RING[msg.axis]
    r = ring_index % size
    if msg.stage == 0:
        return [(0, 0, r)]
    if msg.stage == 1:
        return [(0, r, i1 + j) for j in range(n)]
    return [(r, i2, i1 + j) for j in range(n)]


def simulate(sends, recv_needs, jobs, recv_cost, timers=()):
    done, issued, order = set(), set(), []
    link_free, arrivals = {}, []
    now = 0.0
    ready = []
    jobs = list(jobs)

    def issue():
        for key, (msg, size, needs) in sends.items():
            if key not in issued and needs <= done:
                issued.add(key)
                order.append(("send", key))
                start = max(now, link_free.get(msg.link, 0.0))
                link_free[msg.link] = start + size / RATE
                heapq.heappush(arrivals, (start + size / RATE + LATENCY, key))

    issue()
    timers = list(timers)
    total = len(sends)
    handled = 0
    while handled < total or jobs:
        while timers and timers[0][0] <= now:
            token = timers.pop(0)[1]
            order.append(("job", token))
            done.add(token)
        while arrivals and arrivals[0][0] <= now:
            ready.append(heapq.heappop(arrivals))
        pick = next((r for r in ready if recv_needs[r[1]] <= done), None)
        if pick is not None:
            ready.remove(pick)
            now += recv_cost
            order.append(("recv", pick[1]))
            done.add(("recv",) + pick[1])
            handled += 1
            issue()
            continue
        job = next((j for j in jobs if j[2] <= done), None)
        if job is not None:
            jobs.remove(job)
            now += job[1]
            order.append(("job", job[0]))
            done.add(job[0])
            issue()
            continue
        now = max(now, min([arrivals[0][0]] + [t[0] for t in timers]))
    return order, now


def gather_order():
    msgs = messages()
    source = {}
    for m in msgs:
        for b in blocks_of(m, -m.dist * m.sign):
            source[(m.part,) + b] = ("recv",) + m.key
    sends = {}
    for m in msgs:
        src = blocks_of(m, -(m.dist - 1) * m.sign)
        needs = {source[(m.part,) + b] for b in src if (m.part,) + b in source}
        width = WIDE + (EXTRA if m.part == 0 else 0)
        sends[m.key] = (m, len(src) * ROWS * width * 2, needs)
    jobs = []

    def slab_needs(part, i3s):
        return {v for k, v in source.items() if k[0] == part and k[1] in i3s}

    for part, slabs in GATE_UP_JOBS:
        needs = slab_needs(part, slabs) | {("weights",)}
        jobs.append((("up", part, slabs), 1.0 * len(slabs) if part == 0 else 2.0, needs))
    return sends, simulate(sends, {m.key: set() for m in msgs}, jobs, 0.1, [(22.0, ("weights",))])


GATE_UP_JOBS = (
    (0, (0,)), (1, (0,)), (2, (0,)), (0, (1, 7)), (1, (1,)), (1, (3,)), (2, (1,)), (2, (3,)),
    (0, (2, 6)), (0, (3, 5)), (1, (2,)), (2, (2,)), (0, (4,)),
)
DOWN_JOBS = (
    (0, (4,)), (1, (2,)), (2, (2,)), (0, (3, 5)), (1, (1,)), (2, (1,)), (1, (3,)), (2, (3,)),
    (0, (2, 6)), (0, (1, 7)), (1, (0,)), (2, (0,)), (0, (0,)),
)


def scatter_order():
    msgs = messages()
    by_key = {m.key: m for m in msgs}
    job_of = {}
    for part, slabs in DOWN_JOBS:
        for i3 in slabs:
            job_of[(part, i3)] = ("down", part, slabs)
    adds = {}
    for m in msgs:
        for b in blocks_of(m, (m.dist - 1) * m.sign):
            adds.setdefault((m.part,) + b, []).append(m)
    sends, recv_needs = {}, {}
    for m in msgs:
        src = blocks_of(m, m.dist * m.sign)
        needs = set()
        for b in src:
            needs.add(job_of[(m.part, b[0])])
            for a in adds.get((m.part,) + b, []):
                if a.stage > m.stage or (a.stage == m.stage and a.sign == m.sign and a.dist == m.dist + 1):
                    needs.add(("recv",) + a.key)
        sends[m.key] = (m, len(src) * ROWS * WIDE * 2, needs)
        recv_needs[m.key] = {job_of[(m.part, b[0])] for b in blocks_of(m, (m.dist - 1) * m.sign)}
    jobs = []
    for part, slabs in DOWN_JOBS:
        jobs.append((("down", part, slabs), 0.5 * len(slabs) if part == 0 else 1.0, set()))
    return sends, simulate(sends, recv_needs, jobs, 0.2)


def device_at(x, y, z, core):
    x, y, z = lax.rem(x + 4, 4), lax.rem(y + 4, 4), lax.rem(z + 8, 8)
    return (lax.rem(x, 2), z, (x // 2) * 8 + y * 2 + core)


def kernel(
    tok_ref, gu_ref, dn_ref, ids_ref, gv_ref, old_ref, new_ref, out_ref,
    tok0, tok1, tok2, w_gu, w_dn, acc, hid, xs, hs,
    l30, l20, l10, l31, l21, l11, l32, l22, l12,
    own_sem, w_send, w_recv, ag_send, ag_recv, rs_send, rs_recv,
):
    toks = (tok0, tok1, tok2)
    lands = ((l10, l20, l30), (l11, l21, l31), (l12, l22, l32))
    dp, z, shard = (lax.axis_index(a) for a in AXES)
    core, y, x = lax.rem(shard, 2), lax.rem(shard // 2, 4), (shard // 8) * 2 + dp
    partner = device_at(x, y, z, 1 - core)
    near = {
        ("x", 1): device_at(x + 1, y, z, core), ("x", -1): device_at(x - 1, y, z, core),
        ("y", 1): device_at(x, y + 1, z, core), ("y", -1): device_at(x, y - 1, z, core),
        ("z", 1): device_at(x, y, z + 1, core), ("z", -1): device_at(x, y, z - 1, core),
    }
    mesh_id = pl.DeviceIdType.MESH
    barrier = pltpu.get_barrier_semaphore()
    for dev in (partner, *near.values()):
        pl.semaphore_signal(barrier, inc=1, device_id=dev, device_id_type=mesh_id)

    own = [
        pltpu.make_async_copy(tok_ref.at[:, pl.ds(p * WIDE, WIDE)], toks[p].at[0, 0, 0, :, pl.ds(0, WIDE)], own_sem.at[p])
        for p in range(3)
    ]
    for copy in own:
        copy.start()
    own_w = [
        pltpu.make_async_copy(gu_ref.at[:, 0], w_gu.at[0, 0], own_sem.at[3]),
        pltpu.make_async_copy(gu_ref.at[:, 1], w_gu.at[1, 0], own_sem.at[4]),
        pltpu.make_async_copy(dn_ref, w_dn.at[0], own_sem.at[5]),
    ]
    for copy in own_w:
        copy.start()

    lane = lax.broadcasted_iota(jnp.int32, (ROWS, EXTRA), 1)
    slot = lax.rem(lane, SLOTS)
    held = jnp.zeros((ROWS, EXTRA), jnp.int32)
    for j in range(SLOTS):
        held = jnp.where(slot == j, old_ref[j], held)
    weight = jnp.zeros((ROWS, EXTRA), jnp.float32)
    for k in range(2):
        ids = jnp.broadcast_to(ids_ref[:, k : k + 1], (ROWS, EXTRA))
        gate = jnp.broadcast_to(gv_ref[:, k : k + 1], (ROWS, EXTRA))
        place = jnp.zeros((ROWS, EXTRA), jnp.int32)
        for e in range(SLOTS):
            place = jnp.where(ids == e, new_ref[e], place)
        weight = weight + jnp.where(place == held, gate, 0.0)
    high = weight.astype(jnp.bfloat16).astype(jnp.float32)
    coded = jnp.where(lane < SLOTS, high, jnp.where(lane < 2 * SLOTS, weight - high, 0.0))
    tok0[0, 0, 0, :, WIDE:] = coded.astype(jnp.bfloat16)

    for copy in own:
        copy.wait()
    pl.semaphore_wait(barrier, 7)

    def remote(src, dst, send, recv, dev):
        return pltpu.make_async_remote_copy(
            src_ref=src, dst_ref=dst, send_sem=send, recv_sem=recv, device_id=dev, device_id_type=mesh_id
        )

    def view(msg, ring_index, narrow):
        i3, i2, i1 = blocks_of(msg, ring_index)[0]
        n = subs_of(msg.part, msg.stage)[msg.sub][2]
        ref = toks[msg.part]
        if narrow and msg.part == 0:
            return ref.at[i3, i2, pl.ds(i1, n), :, pl.ds(0, WIDE)]
        return ref.at[i3, i2, pl.ds(i1, n)]

    ag_sends, (ag_order, _) = gather_order()
    index = {key: i for i, key in enumerate(ag_sends)}
    gathers = {}
    for key, (m, _, _) in ag_sends.items():
        gathers[key] = remote(
            view(m, -(m.dist - 1) * m.sign, False), view(m, -m.dist * m.sign, False),
            ag_send.at[index[key]], ag_recv.at[index[key]], near[m.link],
        )
    crossing = [
        remote(gu_ref.at[:, 0], w_gu.at[0, 1], w_send.at[0], w_recv.at[0], partner),
        remote(gu_ref.at[:, 1], w_gu.at[1, 1], w_send.at[1], w_recv.at[1], partner),
        remote(dn_ref, w_dn.at[1], w_send.at[2], w_recv.at[2], partner),
    ]

    def gate_up(part, slabs):
        ref = toks[part]
        for j, i3 in enumerate(slabs):
            n2, n1 = ref.shape[1], ref.shape[2]
            rows = n1 * ROWS
            base = j * n2 * rows

            @pl.loop(0, n2)
            def _(i2):
                block = ref[i3, i2, :, :, pl.ds(0, WIDE)].astype(jnp.float32)
                start = pl.multiple_of(base + i2 * rows, 16)
                xs[pl.ds(start, rows), :] = block.reshape(rows, WIDE).astype(jnp.bfloat16)

        total = 128 * len(slabs) if part == 0 else 256

        @pl.loop(0, 4)
        def _(n):
            half, group = n // 2, lax.rem(n, 2)
            right = w_gu[half, group, :, :, pl.ds(part * WIDE, WIDE)].reshape(SLOTS * SLIVER, WIDE)
            prod = lax.dot_general(
                xs[0:total, :], right, (((1,), (1,)), ((), ())), preferred_element_type=jnp.float32
            )
            cols = pl.ds(pl.multiple_of(n * 256, 256), 256)
            if part == 0:
                for j, i3 in enumerate(slabs):
                    acc[i3, :, :, :, cols] += prod[j * 128 : (j + 1) * 128].reshape(4, 4, ROWS, 256)
            else:
                for i2 in range(4):
                    where = (i2, slabs[0]) if part == 1 else (slabs[0], i2)
                    acc[:, where[0], where[1], :, cols] += prod[i2 * 64 : (i2 + 1) * 64].reshape(8, ROWS, 256)

    crossed = False
    for kind, what in ag_order:
        if kind != "send" and not crossed:
            crossed = True
            for copy in crossing:
                copy.start()
        if kind == "send":
            gathers[what].start()
        elif kind == "recv":
            gathers[what].wait_recv()
        elif what == ("weights",):
            acc[...] = jnp.zeros_like(acc)
            for copy in own_w + crossing:
                copy.wait()
        else:
            gate_up(what[1], what[2])
    for copy in gathers.values():
        copy.wait_send()

    code_row = lax.broadcasted_iota(jnp.int32, (EXTRA, UNITS), 0)
    unit_slot = lax.rem(lax.broadcasted_iota(jnp.int32, (EXTRA, UNITS), 1) // SLIVER, SLOTS)
    spread = jnp.where((code_row < 2 * SLOTS) & (lax.rem(code_row, SLOTS) == unit_slot), 1.0, 0.0)
    spread = spread.astype(jnp.bfloat16)

    @pl.loop(0, 8)
    def _(i3):
        code = tok0[i3, :, :, :, pl.ds(WIDE, EXTRA)].astype(jnp.float32).reshape(128, EXTRA)
        scale = jnp.dot(code.astype(jnp.bfloat16), spread, preferred_element_type=jnp.float32)
        gate = acc[i3, :, :, :, pl.ds(0, UNITS)].reshape(128, UNITS)
        up = acc[i3, :, :, :, pl.ds(UNITS, UNITS)].reshape(128, UNITS)
        value = gate / (1.0 + jnp.exp(-gate)) * up * scale
        hid[i3] = value.reshape(4, 4, ROWS, UNITS)

    def down(part, slabs):
        total = 128 * len(slabs) if part == 0 else 256
        if part == 0:
            for j, i3 in enumerate(slabs):
                hs[j * 128 : (j + 1) * 128, :] = hid[i3].reshape(128, UNITS).astype(jnp.bfloat16)
        else:
            for i2 in range(4):
                where = (i2, slabs[0]) if part == 1 else (slabs[0], i2)
                rows = hid[:, where[0], where[1]].reshape(64, UNITS)
                hs[i2 * 64 : (i2 + 1) * 64, :] = rows.astype(jnp.bfloat16)

        @pl.loop(0, WIDE // 256)
        def _(n):
            cols = pl.ds(pl.multiple_of(part * WIDE + n * 256, 256), 256)
            right = w_dn[:, :, :, cols].reshape(UNITS, 256)
            prod = jnp.dot(hs[0:total, :], right, preferred_element_type=jnp.float32)
            cols = pl.ds(pl.multiple_of(n * 256, 256), 256)
            ref = toks[part]
            n2, n1 = ref.shape[1], ref.shape[2]
            for j, i3 in enumerate(slabs):
                piece = prod[j * 128 : (j + 1) * 128] if part == 0 else prod
                ref[i3, :, :, :, cols] = piece.reshape(n2, n1, ROWS, 256).astype(jnp.bfloat16)

    rs_sends, (rs_order, _) = scatter_order()

    def landing(m):
        return lands[m.part][m.stage].at[0 if m.sign == 1 else 1, m.dist - 1, m.sub]

    scatters = {}
    for key, (m, _, _) in rs_sends.items():
        scatters[key] = remote(
            view(m, m.dist * m.sign, True), landing(m),
            rs_send.at[index[key]], rs_recv.at[index[key]], near[m.link],
        )
    for kind, what in rs_order:
        if kind == "send":
            scatters[what].start()
        elif kind == "job":
            down(what[1], what[2])
        else:
            m = rs_sends[what][0]
            scatters[what].wait_recv()
            target = view(m, (m.dist - 1) * m.sign, True)
            target[...] = target[...] + landing(m)[...]
    for p in range(3):
        out_ref[:, p * WIDE : (p + 1) * WIDE] = toks[p][0, 0, 0, :, 0:WIDE]
    for copy in scatters.values():
        copy.wait_send()


def local(
    tokens, gate_up_weight, down_weight, expert_ids, slot_ids, gate_values, old_place, new_place
):
    count = len(messages())
    bf16, f32 = jnp.bfloat16, jnp.float32
    any_space = pl.BlockSpec(memory_space=pl.ANY)
    vmem = pl.BlockSpec(memory_space=pltpu.VMEM)
    smem = pl.BlockSpec(memory_space=pltpu.SMEM)
    lands = []
    for part in range(3):
        for stage in (2, 1, 0):
            subs = subs_of(part, stage)
            ring = RING[ORDER[part][stage]]
            lands.append(pltpu.VMEM((2, ring // 2, len(subs), subs[0][2], ROWS, WIDE), bf16))
    return pl.pallas_call(
        kernel,
        out_shape=jax.ShapeDtypeStruct((ROWS, 3 * WIDE), bf16),
        in_specs=[any_space, any_space, any_space, vmem, vmem, smem, smem],
        out_specs=vmem,
        scratch_shapes=[
            pltpu.VMEM((8, 4, 4, ROWS, WIDE + EXTRA), bf16),
            pltpu.VMEM((4, 4, 8, ROWS, WIDE), bf16),
            pltpu.VMEM((4, 4, 8, ROWS, WIDE), bf16),
            pltpu.VMEM((2, 2, SLOTS, SLIVER, 3 * WIDE), bf16),
            pltpu.VMEM((2, SLOTS, SLIVER, 3 * WIDE), bf16),
            pltpu.VMEM((8, 4, 4, ROWS, 2 * UNITS), f32),
            pltpu.VMEM((8, 4, 4, ROWS, UNITS), f32),
            pltpu.VMEM((256, WIDE), bf16),
            pltpu.VMEM((256, UNITS), bf16),
            *lands,
            pltpu.SemaphoreType.DMA((6,)),
            pltpu.SemaphoreType.DMA((3,)),
            pltpu.SemaphoreType.DMA((3,)),
            pltpu.SemaphoreType.DMA((count,)),
            pltpu.SemaphoreType.DMA((count,)),
            pltpu.SemaphoreType.DMA((count,)),
            pltpu.SemaphoreType.DMA((count,)),
        ],
        compiler_params=pltpu.CompilerParams(
            collective_id=0, has_side_effects=True, vmem_limit_bytes=67043328
        ),
        name="expert_layer",
    )(tokens, gate_up_weight, down_weight, expert_ids, gate_values, old_place, new_place)


def solution(mesh):
    in_specs = (
        P(AXES, None),
        P(None, None, AXES, None),
        P(None, AXES, None),
        P(AXES, None),
        P(AXES, None),
        P(AXES, None),
        P(),
        P(),
    )
    out_specs = P(AXES, None)
    return jax.shard_map(local, mesh=mesh, in_specs=in_specs, out_specs=out_specs, check_vma=False)
```

```python
import functools
import heapq

import jax
import jax.numpy as jnp
from jax import lax
from jax.experimental import pallas as pl
from jax.experimental.pallas import tpu as pltpu
from jax.sharding import PartitionSpec as P

AXES = ("dp", "expert", "shard")
ROWS = 8
WIDE = 2048
EXTRA = 128
SLOTS = 8
SLIVER = 32
UNITS = 2 * SLOTS * SLIVER
RING = {"x": 4, "y": 4, "z": 8}
ORDER = (("x", "y", "z"), ("z", "y", "x"), ("z", "x", "y"))
RATE, LATENCY = 44500.0, 1.8
AHEAD = 3.0


class Message:
    def __init__(self, part, stage, dist, sign, sub):
        self.part, self.stage, self.dist, self.sign, self.sub = part, stage, dist, sign, sub
        self.key = (part, stage, dist, sign, sub)
        self.axis = ORDER[part][stage]
        self.link = (self.axis, sign)


def position(ring_index, size):
    r = ring_index % size
    return 0 if r == 0 else (2 * r - 1 if r <= size // 2 else 2 * (size - r))


def groups(n1):
    return [(0, 1), (1, 2), (3, 1)] if n1 == 4 else [(0, 1), (1, 2), (3, 2), (5, 3)]


def subs_of(part, stage):
    n1, n2 = RING[ORDER[part][0]], RING[ORDER[part][1]]
    if stage == 0:
        return [(0, 0, 1)]
    first = [(0, i1, n) for i1, n in groups(n1)]
    if stage == 1:
        return first
    rest = [(0, 4)] if n1 == 4 else [(0, 3), (3, 5)]
    return first + [(i2, i1, n) for i2 in range(1, n2) for i1, n in rest]


def far_sign(part, stage, sub):
    subs = subs_of(part, stage)
    if stage == 0:
        return -1 if part == 2 else 1
    if stage == 1:
        return 1 if sub in (0, len(subs) - 1) else -1
    return 1 if subs[sub][0] in (0, 3) else -1


def messages():
    out = []
    for part in range(3):
        for stage in range(3):
            size = RING[ORDER[part][stage]]
            for dist in range(1, size // 2 + 1):
                for sign in (1, -1):
                    for sub in range(len(subs_of(part, stage))):
                        if dist < size // 2 or far_sign(part, stage, sub) == sign:
                            out.append(Message(part, stage, dist, sign, sub))
    return out


def blocks_of(msg, ring_index):
    i2, i1, n = subs_of(msg.part, msg.stage)[msg.sub]
    p = position(ring_index, RING[msg.axis])
    if msg.stage == 0:
        return [(0, 0, p)]
    if msg.stage == 1:
        return [(0, p, i1 + j) for j in range(n)]
    return [(p, i2, i1 + j) for j in range(n)]


def simulate(sends, recv_needs, jobs, recv_cost, timers=(), ahead=AHEAD):
    readers = {}
    for key, (_, _, needs) in sends.items():
        for token in needs:
            readers.setdefault(token, []).append(key)
    tails = {}

    def tail(key):
        if key not in tails:
            after = max((tail(k) for k in readers.get(("recv",) + key, [])), default=0.0)
            tails[key] = sends[key][1] / RATE + LATENCY + after
        return tails[key]

    number = {key: i for i, key in enumerate(sends)}
    missing = {key: len(needs) for key, (_, _, needs) in sends.items()}
    queues, link_free, arrivals = {}, {}, []
    done, order, ready = set(), [], []
    now = 0.0

    def offer(key):
        heapq.heappush(queues.setdefault(sends[key][0].link, []), (-tail(key), number[key], key))

    def finish(token):
        done.add(token)
        for key in readers.get(token, []):
            missing[key] -= 1
            if not missing[key]:
                offer(key)

    def issue():
        for link, queue in queues.items():
            while queue and link_free.get(link, 0.0) - now < ahead:
                key = heapq.heappop(queue)[2]
                order.append(("send", key))
                sent = max(now, link_free.get(link, 0.0)) + sends[key][1] / RATE
                link_free[link] = sent
                heapq.heappush(arrivals, (sent + LATENCY, key))

    for key, count in missing.items():
        if not count:
            offer(key)
    jobs, timers = list(jobs), list(timers)
    handled = 0
    issue()
    while handled < len(sends) or jobs:
        while timers and timers[0][0] <= now:
            token = timers.pop(0)[1]
            order.append(("job", token))
            finish(token)
        while arrivals and arrivals[0][0] <= now:
            ready.append(heapq.heappop(arrivals))
        pick = next((r for r in ready if recv_needs[r[1]] <= done), None)
        job = next((j for j in jobs if j[2] <= done), None)
        if pick is not None:
            ready.remove(pick)
            now += recv_cost
            order.append(("recv", pick[1]))
            finish(("recv",) + pick[1])
            handled += 1
        elif job is not None:
            jobs.remove(job)
            now += job[1]
            order.append(("job", job[0]))
            finish(job[0])
        else:
            times = [a[0] for a in arrivals[:1]] + [t[0] for t in timers[:1]]
            times += [free - ahead + 0.01 for link, free in link_free.items() if queues.get(link)]
            now = max(now, min(times))
        issue()
    return order, now


def gather_order():
    msgs = messages()
    source = {}
    for m in msgs:
        for b in blocks_of(m, -m.dist * m.sign):
            source[(m.part,) + b] = ("recv",) + m.key
    sends = {}
    for m in msgs:
        src = blocks_of(m, -(m.dist - 1) * m.sign)
        needs = {source[(m.part,) + b] for b in src if (m.part,) + b in source}
        width = WIDE + (EXTRA if m.part == 0 else 0)
        sends[m.key] = (m, len(src) * ROWS * width * 2, needs)
    jobs = []
    for part, slabs, low, high in GATE_UP_JOBS:
        needs = {v for k, v in source.items() if k[0] == part and k[1] in slabs and low <= k[2] < high}
        rows = (32 if part == 0 else 64) * (high - low) * len(slabs)
        jobs.append((("up", part, slabs, low, high), UP_COST[rows], needs | {("weights",)}))
    return sends, simulate(sends, {m.key: set() for m in msgs}, jobs, 0.1, [(22.0, ("weights",))])


UP_COST = {128: 1.3, 256: 2.0}
GATE_UP_JOBS = (
    (0, (0,), 0, 4), (1, (0,), 0, 4), (2, (0,), 0, 4), (0, (1, 2), 0, 4), (1, (1,), 0, 4),
    (2, (1,), 0, 4), (1, (2,), 0, 4), (2, (2,), 0, 4), (0, (3, 4), 0, 4), (0, (5, 6), 0, 4),
    (1, (3,), 0, 2), (2, (3,), 0, 2), (1, (3,), 2, 4), (2, (3,), 2, 4), (0, (7,), 0, 4),
)
DOWN_JOBS = (
    ("hid", 0), (0, (7,)), ("hid", 1), (1, (3,)), ("hid", 2), (2, (3,)), ("hid", 3), (0, (5, 6)),
    (1, (1,)), (2, (1,)), (1, (2,)), (2, (2,)), (0, (3, 4)), (0, (1, 2)), (1, (0,)), (2, (0,)), (0, (0,)),
)


def scatter_order():
    msgs = messages()[::-1]
    job_of = {}
    for part, slabs in DOWN_JOBS:
        if part != "hid":
            for i3 in slabs:
                job_of[(part, i3)] = ("down", part, slabs)
    adds = {}
    for m in msgs:
        for b in blocks_of(m, (m.dist - 1) * m.sign):
            adds.setdefault((m.part,) + b, []).append(m)
    sends, recv_needs = {}, {}
    for m in msgs:
        src = blocks_of(m, m.dist * m.sign)
        needs = set()
        for b in src:
            needs.add(job_of[(m.part, b[0])])
            for a in adds.get((m.part,) + b, []):
                if a.stage > m.stage or (a.stage == m.stage and a.sign == m.sign and a.dist == m.dist + 1):
                    needs.add(("recv",) + a.key)
        sends[m.key] = (m, len(src) * ROWS * WIDE * 2, needs)
        recv_needs[m.key] = {job_of[(m.part, b[0])] for b in blocks_of(m, (m.dist - 1) * m.sign)}
    jobs = []
    for part, slabs in DOWN_JOBS:
        if part == "hid":
            jobs.append((("hid", slabs), 0.6, set()))
        else:
            jobs.append((("down", part, slabs), 0.6 * len(slabs) if part == 0 else 1.2, set()))
    return sends, simulate(sends, recv_needs, jobs, 0.2)


def device_at(x, y, z, core):
    x, y, z = lax.rem(x + 4, 4), lax.rem(y + 4, 4), lax.rem(z + 8, 8)
    return (lax.rem(x, 2), z, (x // 2) * 8 + y * 2 + core)


def kernel(
    tok_ref, gu_ref, dn_ref, ids_ref, gv_ref, old_ref, new_ref, out_ref,
    tok0, tok1, tok2, w_gu, w_dn, acc, scale, spread, xs, hs,
    l30, l20, l10, l31, l21, l11, l32, l22, l12,
    own_sem, w_send, w_recv, ag_send, ag_recv, rs_send, rs_recv,
):
    toks = (tok0, tok1, tok2)
    lands = ((l10, l20, l30), (l11, l21, l31), (l12, l22, l32))
    dp, z, shard = (lax.axis_index(a) for a in AXES)
    core, y, x = lax.rem(shard, 2), lax.rem(shard // 2, 4), (shard // 8) * 2 + dp
    partner = device_at(x, y, z, 1 - core)
    near = {
        ("x", 1): device_at(x + 1, y, z, core), ("x", -1): device_at(x - 1, y, z, core),
        ("y", 1): device_at(x, y + 1, z, core), ("y", -1): device_at(x, y - 1, z, core),
        ("z", 1): device_at(x, y, z + 1, core), ("z", -1): device_at(x, y, z - 1, core),
    }
    mesh_id = pl.DeviceIdType.MESH
    barrier = pltpu.get_barrier_semaphore()
    for dev in (partner, *near.values()):
        pl.semaphore_signal(barrier, inc=1, device_id=dev, device_id_type=mesh_id)

    own = [
        pltpu.make_async_copy(tok_ref.at[:, pl.ds(p * WIDE, WIDE)], toks[p].at[0, 0, 0, :, pl.ds(0, WIDE)], own_sem.at[p])
        for p in range(3)
    ]
    for copy in own:
        copy.start()
    own_w = [
        pltpu.make_async_copy(gu_ref.at[:, 0], w_gu.at[0, 0], own_sem.at[3]),
        pltpu.make_async_copy(gu_ref.at[:, 1], w_gu.at[1, 0], own_sem.at[4]),
        pltpu.make_async_copy(dn_ref, w_dn.at[0], own_sem.at[5]),
    ]
    for copy in own_w:
        copy.start()

    lane = lax.broadcasted_iota(jnp.int32, (ROWS, EXTRA), 1)
    slot = lax.rem(lane, SLOTS)
    diagonal = lax.broadcasted_iota(jnp.int32, (ROWS, ROWS), 0) == lax.broadcasted_iota(jnp.int32, (ROWS, ROWS), 1)

    def column(ref, k):
        row = jnp.broadcast_to(ref[k : k + 1, :], (ROWS, ROWS))
        return jnp.sum(jnp.where(diagonal, row, jnp.zeros_like(row)), axis=1, keepdims=True)

    held = jnp.zeros((ROWS, EXTRA), jnp.int32)
    for j in range(SLOTS):
        held = jnp.where(slot == j, old_ref[j], held)
    weight = jnp.zeros((ROWS, EXTRA), jnp.float32)
    for k in range(2):
        ids = jnp.broadcast_to(column(ids_ref, k), (ROWS, EXTRA))
        gate = jnp.broadcast_to(column(gv_ref, k), (ROWS, EXTRA))
        place = jnp.zeros((ROWS, EXTRA), jnp.int32)
        for e in range(SLOTS):
            place = jnp.where(ids == e, new_ref[e], place)
        weight = weight + jnp.where(place == held, gate, 0.0)
    high = weight.astype(jnp.bfloat16).astype(jnp.float32)
    coded = jnp.where(lane < SLOTS, high, jnp.where(lane < 2 * SLOTS, weight - high, 0.0))
    tok0[0, 0, 0, :, WIDE:] = coded.astype(jnp.bfloat16)

    for copy in own:
        copy.wait()
    pl.semaphore_wait(barrier, 7)

    def remote(src, dst, send, recv, dev):
        return pltpu.make_async_remote_copy(
            src_ref=src, dst_ref=dst, send_sem=send, recv_sem=recv, device_id=dev, device_id_type=mesh_id
        )

    def view(msg, ring_index, narrow):
        i3, i2, i1 = blocks_of(msg, ring_index)[0]
        n = subs_of(msg.part, msg.stage)[msg.sub][2]
        ref = toks[msg.part]
        if narrow and msg.part == 0:
            return ref.at[i3, i2, pl.ds(i1, n), :, pl.ds(0, WIDE)]
        return ref.at[i3, i2, pl.ds(i1, n)]

    ag_sends, (ag_order, _) = gather_order()
    index = {key: i for i, key in enumerate(ag_sends)}
    gathers = {}
    for key, (m, _, _) in ag_sends.items():
        gathers[key] = remote(
            view(m, -(m.dist - 1) * m.sign, False), view(m, -m.dist * m.sign, False),
            ag_send.at[index[key]], ag_recv.at[index[key]], near[m.link],
        )
    crossing = [
        remote(gu_ref.at[:, 0], w_gu.at[0, 1], w_send.at[0], w_recv.at[0], partner),
        remote(gu_ref.at[:, 1], w_gu.at[1, 1], w_send.at[1], w_recv.at[1], partner),
        remote(dn_ref, w_dn.at[1], w_send.at[2], w_recv.at[2], partner),
    ]

    def gate_up(part, slabs, low, high):
        ref = toks[part]
        count, rows = high - low, ref.shape[2] * ROWS
        for j, i3 in enumerate(slabs):

            @pl.loop(0, count)
            def _(i2):
                block = ref[i3, low + i2, :, :, pl.ds(0, WIDE)].astype(jnp.float32)
                start = pl.multiple_of((j * count + i2) * rows, 16)
                xs[pl.ds(start, rows), :] = block.reshape(rows, WIDE).astype(jnp.bfloat16)

        total = count * rows * len(slabs)

        @pl.loop(0, 4)
        def _(n):
            half, group = n // 2, lax.rem(n, 2)
            right = w_gu[half, group, :, :, pl.ds(part * WIDE, WIDE)].reshape(SLOTS * SLIVER, WIDE)
            prod = lax.dot_general(
                xs[0:total, :], right, (((1,), (1,)), ((), ())), preferred_element_type=jnp.float32
            )
            cols = pl.ds(pl.multiple_of(n * 256, 256), 256)
            if part == 0:
                for j, i3 in enumerate(slabs):
                    acc[i3, :, :, :, cols] += prod[j * 128 : (j + 1) * 128].reshape(4, 4, ROWS, 256)
            else:
                for i2 in range(count):
                    where = (low + i2, slabs[0]) if part == 1 else (slabs[0], low + i2)
                    acc[:, where[0], where[1], :, cols] += prod[i2 * 64 : (i2 + 1) * 64].reshape(8, ROWS, 256)

        if part == 0:
            for i3 in slabs:
                code = tok0[i3, :, :, :, pl.ds(WIDE, EXTRA)].astype(jnp.float32).reshape(128, EXTRA)
                wide = jnp.dot(code.astype(jnp.bfloat16), spread[...], preferred_element_type=jnp.float32)
                scale[i3] = wide.reshape(4, 4, ROWS, UNITS)

    crossed = False
    for kind, what in ag_order:
        if kind != "send" and not crossed:
            crossed = True
            for copy in crossing:
                copy.start()
        if kind == "send":
            gathers[what].start()
        elif kind == "recv":
            gathers[what].wait_recv()
        elif what == ("weights",):
            acc[...] = jnp.zeros_like(acc)
            code_row = lax.broadcasted_iota(jnp.int32, (EXTRA, UNITS), 0)
            unit_slot = lax.rem(lax.broadcasted_iota(jnp.int32, (EXTRA, UNITS), 1) // SLIVER, SLOTS)
            chosen = (code_row < 2 * SLOTS) & (lax.rem(code_row, SLOTS) == unit_slot)
            spread[...] = jnp.where(chosen, 1.0, 0.0).astype(jnp.bfloat16)
            for copy in own_w + crossing:
                copy.wait()
        else:
            gate_up(*what[1:])
    for copy in gathers.values():
        copy.wait_send()

    def hidden(where):
        gate = acc[(*where, slice(None), pl.ds(0, UNITS))]
        up = acc[(*where, slice(None), pl.ds(UNITS, UNITS))]
        acc[(*where, slice(None), pl.ds(0, UNITS))] = (
            gate / (1.0 + jnp.exp(-gate)) * up * scale[(*where, slice(None), slice(None))]
        )

    def hidden_rows(step):
        if step == 0:
            pl.loop(0, 4)(lambda i: hidden((7, i, slice(None))))
        elif step == 1:
            pl.loop(0, 7)(lambda i: hidden((i, slice(None), 3)))
        elif step == 2:
            pl.loop(0, 7)(lambda i: hidden((i, 3, pl.ds(0, 3))))
        else:
            pl.loop(0, 21)(lambda i: hidden((i // 3, lax.rem(i, 3), pl.ds(0, 3))))

    def down(part, slabs):
        total = 128 * len(slabs) if part == 0 else 256
        if part == 0:
            for j, i3 in enumerate(slabs):
                hs[j * 128 : (j + 1) * 128, :] = acc[i3, :, :, :, pl.ds(0, UNITS)].reshape(128, UNITS).astype(jnp.bfloat16)
        else:
            for i2 in range(4):
                where = (i2, slabs[0]) if part == 1 else (slabs[0], i2)
                rows = acc[:, where[0], where[1], :, pl.ds(0, UNITS)].reshape(64, UNITS)
                hs[i2 * 64 : (i2 + 1) * 64, :] = rows.astype(jnp.bfloat16)

        @pl.loop(0, WIDE // 256)
        def _(n):
            cols = pl.ds(pl.multiple_of(part * WIDE + n * 256, 256), 256)
            right = w_dn[:, :, :, cols].reshape(UNITS, 256)
            prod = jnp.dot(hs[0:total, :], right, preferred_element_type=jnp.float32)
            cols = pl.ds(pl.multiple_of(n * 256, 256), 256)
            ref = toks[part]
            n2, n1 = ref.shape[1], ref.shape[2]
            for j, i3 in enumerate(slabs):
                piece = prod[j * 128 : (j + 1) * 128] if part == 0 else prod
                ref[i3, :, :, :, cols] = piece.reshape(n2, n1, ROWS, 256).astype(jnp.bfloat16)

    rs_sends, (rs_order, _) = scatter_order()

    def landing(m):
        i2, i1, n = subs_of(m.part, m.stage)[m.sub]
        return lands[m.part][m.stage].at[0 if m.sign == 1 else 1, m.dist - 1, i2, pl.ds(i1, n)]

    scatters = {}
    for key, (m, _, _) in rs_sends.items():
        scatters[key] = remote(
            view(m, m.dist * m.sign, True), landing(m),
            rs_send.at[index[key]], rs_recv.at[index[key]], near[m.link],
        )
    for kind, what in rs_order:
        if kind == "send":
            scatters[what].start()
        elif kind == "job" and what[0] == "hid":
            hidden_rows(what[1])
        elif kind == "job":
            down(what[1], what[2])
        else:
            m = rs_sends[what][0]
            scatters[what].wait_recv()
            target = view(m, (m.dist - 1) * m.sign, True)
            target[...] = target[...] + landing(m)[...]
    for p in range(3):
        out_ref[:, p * WIDE : (p + 1) * WIDE] = toks[p][0, 0, 0, :, 0:WIDE]
    for copy in scatters.values():
        copy.wait_send()


def local(
    tokens, gate_up_weight, down_weight, expert_ids, slot_ids, gate_values, old_place, new_place
):
    count = len(messages())
    bf16, f32 = jnp.bfloat16, jnp.float32
    any_space = pl.BlockSpec(memory_space=pl.ANY)
    vmem = pl.BlockSpec(memory_space=pltpu.VMEM)
    smem = pl.BlockSpec(memory_space=pltpu.SMEM)
    lands = []
    for part in range(3):
        for stage in (2, 1, 0):
            n1, n2, _ = (RING[axis] for axis in ORDER[part])
            ring = RING[ORDER[part][stage]]
            shape = (n2 if stage == 2 else 1, n1 if stage else 1)
            lands.append(pltpu.VMEM((2, ring // 2, *shape, ROWS, WIDE), bf16))
    return pl.pallas_call(
        kernel,
        out_shape=jax.ShapeDtypeStruct((ROWS, 3 * WIDE), bf16),
        in_specs=[any_space, any_space, any_space, vmem, vmem, smem, smem],
        out_specs=vmem,
        scratch_shapes=[
            pltpu.VMEM((8, 4, 4, ROWS, WIDE + EXTRA), bf16),
            pltpu.VMEM((4, 4, 8, ROWS, WIDE), bf16),
            pltpu.VMEM((4, 4, 8, ROWS, WIDE), bf16),
            pltpu.VMEM((2, 2, SLOTS, SLIVER, 3 * WIDE), bf16),
            pltpu.VMEM((2, SLOTS, SLIVER, 3 * WIDE), bf16),
            pltpu.VMEM((8, 4, 4, ROWS, 2 * UNITS), f32),
            pltpu.VMEM((8, 4, 4, ROWS, UNITS), f32),
            pltpu.VMEM((EXTRA, UNITS), bf16),
            pltpu.VMEM((256, WIDE), bf16),
            pltpu.VMEM((256, UNITS), bf16),
            *lands,
            pltpu.SemaphoreType.DMA((6,)),
            pltpu.SemaphoreType.DMA((3,)),
            pltpu.SemaphoreType.DMA((3,)),
            pltpu.SemaphoreType.DMA((count,)),
            pltpu.SemaphoreType.DMA((count,)),
            pltpu.SemaphoreType.DMA((count,)),
            pltpu.SemaphoreType.DMA((count,)),
        ],
        compiler_params=pltpu.CompilerParams(
            collective_id=0, has_side_effects=True, vmem_limit_bytes=67043328
        ),
        name="expert_layer",
    )(tokens, gate_up_weight, down_weight, expert_ids.T, gate_values.T, old_place, new_place)


def solution(mesh):
    in_specs = (
        P(AXES, None),
        P(None, None, AXES, None),
        P(None, AXES, None),
        P(AXES, None),
        P(AXES, None),
        P(AXES, None),
        P(),
        P(),
    )
    out_specs = P(AXES, None)
    return jax.shard_map(local, mesh=mesh, in_specs=in_specs, out_specs=out_specs, check_vma=False)
```

```python
import functools
import heapq

import jax
import jax.numpy as jnp
from jax import lax
from jax.experimental import pallas as pl
from jax.experimental.pallas import tpu as pltpu
from jax.sharding import PartitionSpec as P

AXES = ("dp", "expert", "shard")
ROWS = 8
WIDE = 2048
EXTRA = 128
SLOTS = 8
SLIVER = 32
UNITS = 2 * SLOTS * SLIVER
RING = {"x": 4, "y": 4, "z": 8}
ORDER = (("x", "y", "z"), ("z", "y", "x"), ("z", "x", "y"))
RATE, LATENCY = 44500.0, 1.8
AHEAD = 3.0
GATHER_BONUS = {(2, 1): 2.1, (2, 2): 8.3, (1, 1): 12.7, (0, 2): 9.2, (0, 0): 12.6, (0, 1): -0.2, (1, 2): 11.2, (1, 0): 5.2, (2, 0): 5.8}
SCATTER_BONUS = {(0, 0): -6.3, (2, 0): 13.8, (1, 0): 10.2, (1, 1): 9.9, (1, 2): -3.4, (0, 1): -1.4, (2, 1): -2.5, (0, 2): 5.3, (2, 2): -1.7}


class Message:
    def __init__(self, part, stage, dist, sign, sub):
        self.part, self.stage, self.dist, self.sign, self.sub = part, stage, dist, sign, sub
        self.key = (part, stage, dist, sign, sub)
        self.axis = ORDER[part][stage]
        self.link = (self.axis, sign)


def position(ring_index, size):
    r = ring_index % size
    return 0 if r == 0 else (2 * r - 1 if r <= size // 2 else 2 * (size - r))


def groups(n1):
    return [(0, 1), (1, 2), (3, 1)] if n1 == 4 else [(0, 1), (1, 2), (3, 2), (5, 3)]


def subs_of(part, stage):
    n1, n2 = RING[ORDER[part][0]], RING[ORDER[part][1]]
    if stage == 0:
        return [(0, 0, 1)]
    first = [(0, i1, n) for i1, n in groups(n1)]
    if stage == 1:
        return first
    rest = [(0, 4)] if n1 == 4 else [(0, 3), (3, 5)]
    return first + [(i2, i1, n) for i2 in range(1, n2) for i1, n in rest]


def far_sign(part, stage, sub):
    subs = subs_of(part, stage)
    if stage == 0:
        return -1 if part == 2 else 1
    if stage == 1:
        return 1 if sub in (0, len(subs) - 1) else -1
    return 1 if subs[sub][0] in (0, 3) else -1


def messages():
    out = []
    for part in range(3):
        for stage in range(3):
            size = RING[ORDER[part][stage]]
            for dist in range(1, size // 2 + 1):
                for sign in (1, -1):
                    for sub in range(len(subs_of(part, stage))):
                        if dist < size // 2 or far_sign(part, stage, sub) == sign:
                            out.append(Message(part, stage, dist, sign, sub))
    return out


def blocks_of(msg, ring_index):
    i2, i1, n = subs_of(msg.part, msg.stage)[msg.sub]
    p = position(ring_index, RING[msg.axis])
    if msg.stage == 0:
        return [(0, 0, p)]
    if msg.stage == 1:
        return [(0, p, i1 + j) for j in range(n)]
    return [(p, i2, i1 + j) for j in range(n)]


def simulate(sends, recv_needs, jobs, recv_cost, timers=(), ahead=AHEAD, bonus=None):
    readers = {}
    for key, (_, _, needs) in sends.items():
        for token in needs:
            readers.setdefault(token, []).append(key)
    tails = {}

    def tail(key):
        if key not in tails:
            after = max((tail(k) for k in readers.get(("recv",) + key, [])), default=0.0)
            tails[key] = sends[key][1] / RATE + LATENCY + after
        return tails[key]

    number = {key: i for i, key in enumerate(sends)}
    missing = {key: len(needs) for key, (_, _, needs) in sends.items()}
    queues, link_free, arrivals = {}, {}, []
    done, order, ready = set(), [], []
    now = 0.0

    def offer(key):
        rank = tail(key) + (bonus or {}).get(key[:2], 0.0)
        heapq.heappush(queues.setdefault(sends[key][0].link, []), (-rank, number[key], key))

    def finish(token):
        done.add(token)
        for key in readers.get(token, []):
            missing[key] -= 1
            if not missing[key]:
                offer(key)

    def issue():
        for link, queue in queues.items():
            while queue and link_free.get(link, 0.0) - now < ahead:
                key = heapq.heappop(queue)[2]
                order.append(("send", key))
                sent = max(now, link_free.get(link, 0.0)) + sends[key][1] / RATE
                link_free[link] = sent
                heapq.heappush(arrivals, (sent + LATENCY, key))

    for key, count in missing.items():
        if not count:
            offer(key)
    jobs, timers = list(jobs), list(timers)
    handled = 0
    issue()
    while handled < len(sends) or jobs:
        while timers and timers[0][0] <= now:
            token = timers.pop(0)[1]
            order.append(("job", token))
            finish(token)
        while arrivals and arrivals[0][0] <= now:
            ready.append(heapq.heappop(arrivals))
        pick = next((r for r in ready if recv_needs[r[1]] <= done), None)
        job = next((j for j in jobs if j[2] <= done), None)
        if pick is not None:
            ready.remove(pick)
            now += recv_cost
            order.append(("recv", pick[1]))
            finish(("recv",) + pick[1])
            handled += 1
        elif job is not None:
            jobs.remove(job)
            now += job[1]
            order.append(("job", job[0]))
            finish(job[0])
        else:
            times = [a[0] for a in arrivals[:1]] + [t[0] for t in timers[:1]]
            times += [free - ahead + 0.01 for link, free in link_free.items() if queues.get(link)]
            now = max(now, min(times))
        issue()
    return order, now


def gather_order():
    msgs = messages()
    source = {}
    for m in msgs:
        for b in blocks_of(m, -m.dist * m.sign):
            source[(m.part,) + b] = ("recv",) + m.key
    sends = {}
    for m in msgs:
        src = blocks_of(m, -(m.dist - 1) * m.sign)
        needs = {source[(m.part,) + b] for b in src if (m.part,) + b in source}
        width = WIDE + (EXTRA if m.part == 0 else 0)
        sends[m.key] = (m, len(src) * ROWS * width * 2, needs)
    jobs = []
    for part, slabs, i2s, held in GATE_UP_JOBS:
        needs = {v for k, v in source.items() if k[0] == part and k[1] in slabs and k[2] in i2s}
        rows = (32 if part == 0 else 64) * len(i2s) * len(slabs)
        cost = UP_COST[rows] * len(held)
        jobs.append((("up", part, slabs, i2s, held), cost, needs | {("weights", held[-1])}))
    timers = [(OWN_AT, ("weights", 0)), (PARTNER_AT, ("weights", 1))]
    return sends, simulate(sends, {m.key: set() for m in msgs}, jobs, 0.1, timers, bonus=GATHER_BONUS)


OWN_AT, PARTNER_AT = 5.0, 20.0
UP_COST = {64: 0.75, 128: 0.8, 192: 0.85, 256: 0.9, 384: 1.3}
HIDDEN_COST = (0.8, 0.4, 0.7, 1.5)
ALL = (0, 1, 2, 3)
GATE_UP_JOBS = (
    (1, (3,), ALL, (0, 1)),
    (1, (1,), (0,), (0, 1)),
    (0, (7,), ALL, (0, 1)),
    (0, (0, 1, 2), ALL, (0, 1)),
    (1, (2,), (1, 2, 3), (0, 1)),
    (1, (2,), (0,), (0, 1)),
    (2, (0,), ALL, (0, 1)),
    (1, (0,), (2, 3), (0, 1)),
    (2, (2,), ALL, (0, 1)),
    (1, (0,), (0, 1), (0, 1)),
    (2, (1,), (0, 1), (0, 1)),
    (2, (1,), (2, 3), (0, 1)),
    (2, (3,), ALL, (0, 1)),
    (1, (1,), (1, 2, 3), (0, 1)),
    (0, (3, 4), ALL, (0, 1)),
    (0, (5, 6), ALL, (0, 1)),
)
DOWN_JOBS = (
    ("hid", 0), (2, (3,)), ("hid", 1), (0, (7,)), ("hid", 2), (1, (3,)),
    ("hid", 3), (0, (5, 6)), (1, (1,)), (2, (1,)), (2, (2,)), (0, (3, 4)),
    (1, (2,)), (2, (0,)), (0, (0,)), (1, (0,)), (0, (1, 2)),
)


def scatter_order():
    msgs = messages()[::-1]
    job_of = {}
    for part, slabs in DOWN_JOBS:
        if part != "hid":
            for i3 in slabs:
                job_of[(part, i3)] = ("down", part, slabs)
    adds = {}
    for m in msgs:
        for b in blocks_of(m, (m.dist - 1) * m.sign):
            adds.setdefault((m.part,) + b, []).append(m)
    sends, recv_needs = {}, {}
    for m in msgs:
        src = blocks_of(m, m.dist * m.sign)
        needs = set()
        for b in src:
            needs.add(job_of[(m.part, b[0])])
            for a in adds.get((m.part,) + b, []):
                if a.stage > m.stage or (a.stage == m.stage and a.sign == m.sign and a.dist == m.dist + 1):
                    needs.add(("recv",) + a.key)
        sends[m.key] = (m, len(src) * ROWS * WIDE * 2, needs)
        recv_needs[m.key] = {job_of[(m.part, b[0])] for b in blocks_of(m, (m.dist - 1) * m.sign)}
    jobs = []
    for part, slabs in DOWN_JOBS:
        if part == "hid":
            jobs.append((("hid", slabs), HIDDEN_COST[slabs], set()))
        else:
            jobs.append((("down", part, slabs), 0.75 * len(slabs) if part == 0 else 1.1, set()))
    return sends, simulate(sends, recv_needs, jobs, 0.2, bonus=SCATTER_BONUS)


def device_at(x, y, z, core):
    x, y, z = lax.rem(x + 4, 4), lax.rem(y + 4, 4), lax.rem(z + 8, 8)
    return (lax.rem(x, 2), z, (x // 2) * 8 + y * 2 + core)


def kernel(
    tok_ref, gu_ref, dn_ref, ids_ref, gv_ref, old_ref, new_ref, out_ref,
    tok0, tok1, tok2, w_gu, w_dn, acc, scale, spread, xs, hs,
    l30, l20, l10, l31, l21, l11, l32, l22, l12,
    own_sem, w_send, w_recv, ag_send, ag_recv, rs_send, rs_recv,
):
    toks = (tok0, tok1, tok2)
    lands = ((l10, l20, l30), (l11, l21, l31), (l12, l22, l32))
    dp, z, shard = (lax.axis_index(a) for a in AXES)
    core, y, x = lax.rem(shard, 2), lax.rem(shard // 2, 4), (shard // 8) * 2 + dp
    partner = device_at(x, y, z, 1 - core)
    near = {
        ("x", 1): device_at(x + 1, y, z, core), ("x", -1): device_at(x - 1, y, z, core),
        ("y", 1): device_at(x, y + 1, z, core), ("y", -1): device_at(x, y - 1, z, core),
        ("z", 1): device_at(x, y, z + 1, core), ("z", -1): device_at(x, y, z - 1, core),
    }
    mesh_id = pl.DeviceIdType.MESH
    barrier = pltpu.get_barrier_semaphore()
    for dev in (partner, *near.values()):
        pl.semaphore_signal(barrier, inc=1, device_id=dev, device_id_type=mesh_id)

    own = [
        pltpu.make_async_copy(tok_ref.at[:, pl.ds(p * WIDE, WIDE)], toks[p].at[0, 0, 0, :, pl.ds(0, WIDE)], own_sem.at[p])
        for p in range(3)
    ]
    for copy in own:
        copy.start()
    own_w = [
        pltpu.make_async_copy(gu_ref.at[:, 0], w_gu.at[0, 0], own_sem.at[3]),
        pltpu.make_async_copy(gu_ref.at[:, 1], w_gu.at[0, 1], own_sem.at[4]),
        pltpu.make_async_copy(dn_ref, w_dn.at[0], own_sem.at[5]),
    ]
    for copy in own_w:
        copy.start()

    lane = lax.broadcasted_iota(jnp.int32, (ROWS, EXTRA), 1)
    slot = lax.rem(lane, SLOTS)
    diagonal = lax.broadcasted_iota(jnp.int32, (ROWS, ROWS), 0) == lax.broadcasted_iota(jnp.int32, (ROWS, ROWS), 1)

    def column(ref, k):
        row = jnp.broadcast_to(ref[k : k + 1, :], (ROWS, ROWS))
        return jnp.sum(jnp.where(diagonal, row, jnp.zeros_like(row)), axis=1, keepdims=True)

    held = jnp.zeros((ROWS, EXTRA), jnp.int32)
    for j in range(SLOTS):
        held = jnp.where(slot == j, old_ref[j], held)
    weight = jnp.zeros((ROWS, EXTRA), jnp.float32)
    for k in range(2):
        ids = jnp.broadcast_to(column(ids_ref, k), (ROWS, EXTRA))
        gate = jnp.broadcast_to(column(gv_ref, k), (ROWS, EXTRA))
        place = jnp.zeros((ROWS, EXTRA), jnp.int32)
        for e in range(SLOTS):
            place = jnp.where(ids == e, new_ref[e], place)
        weight = weight + jnp.where(place == held, gate, 0.0)
    high = weight.astype(jnp.bfloat16).astype(jnp.float32)
    coded = jnp.where(lane < SLOTS, high, jnp.where(lane < 2 * SLOTS, weight - high, 0.0))
    tok0[0, 0, 0, :, WIDE:] = coded.astype(jnp.bfloat16)

    for copy in own:
        copy.wait()
    pl.semaphore_wait(barrier, 7)

    def remote(src, dst, send, recv, dev):
        return pltpu.make_async_remote_copy(
            src_ref=src, dst_ref=dst, send_sem=send, recv_sem=recv, device_id=dev, device_id_type=mesh_id
        )

    def view(msg, ring_index, narrow):
        i3, i2, i1 = blocks_of(msg, ring_index)[0]
        n = subs_of(msg.part, msg.stage)[msg.sub][2]
        ref = toks[msg.part]
        if narrow and msg.part == 0:
            return ref.at[i3, i2, pl.ds(i1, n), :, pl.ds(0, WIDE)]
        return ref.at[i3, i2, pl.ds(i1, n)]

    ag_sends, (ag_order, _) = gather_order()
    index = {key: i for i, key in enumerate(ag_sends)}
    gathers = {}
    for key, (m, _, _) in ag_sends.items():
        gathers[key] = remote(
            view(m, -(m.dist - 1) * m.sign, False), view(m, -m.dist * m.sign, False),
            ag_send.at[index[key]], ag_recv.at[index[key]], near[m.link],
        )
    crossing = [
        remote(gu_ref.at[:, 0], w_gu.at[1, 0], w_send.at[0], w_recv.at[0], partner),
        remote(gu_ref.at[:, 1], w_gu.at[1, 1], w_send.at[1], w_recv.at[1], partner),
        remote(dn_ref, w_dn.at[1], w_send.at[2], w_recv.at[2], partner),
    ]

    def gate_up(part, slabs, i2s, held):
        ref = toks[part]
        count, rows = len(i2s), ref.shape[2] * ROWS
        step = i2s[1] - i2s[0] if count > 1 else 1
        for j, i3 in enumerate(slabs):

            @pl.loop(0, count)
            def _(i2):
                block = ref[i3, i2s[0] + step * i2, :, :, pl.ds(0, WIDE)].astype(jnp.float32)
                start = pl.multiple_of((j * count + i2) * rows, 16)
                xs[pl.ds(start, rows), :] = block.reshape(rows, WIDE).astype(jnp.bfloat16)

        total = count * rows * len(slabs)

        @pl.loop(held[0], held[-1] + 1)
        def _(group):
            right = w_gu[group, :, :, :, pl.ds(part * WIDE, WIDE)].reshape(UNITS, WIDE)
            prod = lax.dot_general(
                xs[0:total, :], right, (((1,), (1,)), ((), ())), preferred_element_type=jnp.float32
            )
            cols = pl.ds(pl.multiple_of(group * UNITS, UNITS), UNITS)
            if part == 0:
                for j, i3 in enumerate(slabs):
                    acc[i3, :, :, :, cols] += prod[j * 128 : (j + 1) * 128].reshape(4, 4, ROWS, UNITS)
            else:
                for i2 in range(count):
                    where = (i2s[i2], slabs[0]) if part == 1 else (slabs[0], i2s[i2])
                    acc[:, where[0], where[1], :, cols] += prod[i2 * 64 : (i2 + 1) * 64].reshape(8, ROWS, UNITS)

        if part == 0 and held[-1] == 1:
            for i3 in slabs:
                code = tok0[i3, :, :, :, pl.ds(WIDE, EXTRA)].astype(jnp.float32).reshape(128, EXTRA)
                wide = jnp.dot(code.astype(jnp.bfloat16), spread[...], preferred_element_type=jnp.float32)
                scale[i3] = wide.reshape(4, 4, ROWS, UNITS)

    crossed = False
    for kind, what in ag_order:
        if kind != "send" and not crossed:
            crossed = True
            for copy in crossing:
                copy.start()
            acc[...] = jnp.zeros_like(acc)
            code_row = lax.broadcasted_iota(jnp.int32, (EXTRA, UNITS), 0)
            unit_slot = lax.rem(lax.broadcasted_iota(jnp.int32, (EXTRA, UNITS), 1) // SLIVER, SLOTS)
            chosen = (code_row < 2 * SLOTS) & (lax.rem(code_row, SLOTS) == unit_slot)
            spread[...] = jnp.where(chosen, 1.0, 0.0).astype(jnp.bfloat16)
        if kind == "send":
            gathers[what].start()
        elif kind == "recv":
            gathers[what].wait_recv()
        elif what == ("weights", 1):
            for copy in crossing:
                copy.wait()
        elif what == ("weights", 0):
            for copy in own_w:
                copy.wait()
        else:
            gate_up(*what[1:])
    for copy in gathers.values():
        copy.wait_send()

    def hidden(where):
        width = UNITS // 2
        values = []
        for group in range(2):
            gate = acc[(*where, slice(None), pl.ds(group * UNITS, width))]
            up = acc[(*where, slice(None), pl.ds(group * UNITS + width, width))]
            share = scale[(*where, slice(None), pl.ds(group * width, width))]
            values.append(gate / (1.0 + jnp.exp(-gate)) * up * share)
        for group in range(2):
            acc[(*where, slice(None), pl.ds(group * width, width))] = values[group]

    def hidden_rows(step):
        if step == 0:
            pl.loop(0, 8)(lambda i: hidden((i, 3, slice(None))))
        elif step == 1:
            pl.loop(0, 3)(lambda i: hidden((7, i, slice(None))))
        elif step == 2:
            pl.loop(0, 7)(lambda i: hidden((i, pl.ds(0, 3), 3)))
        else:
            pl.loop(0, 21)(lambda i: hidden((i // 3, lax.rem(i, 3), pl.ds(0, 3))))

    def down(part, slabs):
        total = 128 * len(slabs) if part == 0 else 256
        if part == 0:
            for j, i3 in enumerate(slabs):
                hs[j * 128 : (j + 1) * 128, :] = acc[i3, :, :, :, pl.ds(0, UNITS)].reshape(128, UNITS).astype(jnp.bfloat16)
        else:
            for i2 in range(4):
                where = (i2, slabs[0]) if part == 1 else (slabs[0], i2)
                rows = acc[:, where[0], where[1], :, pl.ds(0, UNITS)].reshape(64, UNITS)
                hs[i2 * 64 : (i2 + 1) * 64, :] = rows.astype(jnp.bfloat16)

        @pl.loop(0, WIDE // 512)
        def _(n):
            cols = pl.ds(pl.multiple_of(part * WIDE + n * 512, 512), 512)
            right = w_dn[:, :, :, cols].reshape(UNITS, 512)
            prod = jnp.dot(hs[0:total, :], right, preferred_element_type=jnp.float32)
            cols = pl.ds(pl.multiple_of(n * 512, 512), 512)
            ref = toks[part]
            n2, n1 = ref.shape[1], ref.shape[2]
            for j, i3 in enumerate(slabs):
                piece = prod[j * 128 : (j + 1) * 128] if part == 0 else prod
                ref[i3, :, :, :, cols] = piece.reshape(n2, n1, ROWS, 512).astype(jnp.bfloat16)

    rs_sends, (rs_order, _) = scatter_order()

    def landing(m):
        i2, i1, n = subs_of(m.part, m.stage)[m.sub]
        return lands[m.part][m.stage].at[0 if m.sign == 1 else 1, m.dist - 1, i2, pl.ds(i1, n)]

    scatters = {}
    for key, (m, _, _) in rs_sends.items():
        scatters[key] = remote(
            view(m, m.dist * m.sign, True), landing(m),
            rs_send.at[index[key]], rs_recv.at[index[key]], near[m.link],
        )
    for kind, what in rs_order:
        if kind == "send":
            scatters[what].start()
        elif kind == "job" and what[0] == "hid":
            hidden_rows(what[1])
        elif kind == "job":
            down(what[1], what[2])
        else:
            m = rs_sends[what][0]
            scatters[what].wait_recv()
            target = view(m, (m.dist - 1) * m.sign, True)
            target[...] = target[...] + landing(m)[...]
    for p in range(3):
        out_ref[:, p * WIDE : (p + 1) * WIDE] = toks[p][0, 0, 0, :, 0:WIDE]
    for copy in scatters.values():
        copy.wait_send()


def local(
    tokens, gate_up_weight, down_weight, expert_ids, slot_ids, gate_values, old_place, new_place
):
    count = len(messages())
    bf16, f32 = jnp.bfloat16, jnp.float32
    any_space = pl.BlockSpec(memory_space=pl.ANY)
    vmem = pl.BlockSpec(memory_space=pltpu.VMEM)
    smem = pl.BlockSpec(memory_space=pltpu.SMEM)
    lands = []
    for part in range(3):
        for stage in (2, 1, 0):
            n1, n2, _ = (RING[axis] for axis in ORDER[part])
            ring = RING[ORDER[part][stage]]
            shape = (n2 if stage == 2 else 1, n1 if stage else 1)
            lands.append(pltpu.VMEM((2, ring // 2, *shape, ROWS, WIDE), bf16))
    return pl.pallas_call(
        kernel,
        out_shape=jax.ShapeDtypeStruct((ROWS, 3 * WIDE), bf16),
        in_specs=[any_space, any_space, any_space, vmem, vmem, smem, smem],
        out_specs=vmem,
        scratch_shapes=[
            pltpu.VMEM((8, 4, 4, ROWS, WIDE + EXTRA), bf16),
            pltpu.VMEM((4, 4, 8, ROWS, WIDE), bf16),
            pltpu.VMEM((4, 4, 8, ROWS, WIDE), bf16),
            pltpu.VMEM((2, 2, SLOTS, SLIVER, 3 * WIDE), bf16),
            pltpu.VMEM((2, SLOTS, SLIVER, 3 * WIDE), bf16),
            pltpu.VMEM((8, 4, 4, ROWS, 2 * UNITS), f32),
            pltpu.VMEM((8, 4, 4, ROWS, UNITS), f32),
            pltpu.VMEM((EXTRA, UNITS), bf16),
            pltpu.VMEM((384, WIDE), bf16),
            pltpu.VMEM((256, UNITS), bf16),
            *lands,
            pltpu.SemaphoreType.DMA((6,)),
            pltpu.SemaphoreType.DMA((3,)),
            pltpu.SemaphoreType.DMA((3,)),
            pltpu.SemaphoreType.DMA((count,)),
            pltpu.SemaphoreType.DMA((count,)),
            pltpu.SemaphoreType.DMA((count,)),
            pltpu.SemaphoreType.DMA((count,)),
        ],
        compiler_params=pltpu.CompilerParams(
            collective_id=0, has_side_effects=True, vmem_limit_bytes=67043328
        ),
        name="expert_layer",
    )(tokens, gate_up_weight, down_weight, expert_ids.T, gate_values.T, old_place, new_place)


def solution(mesh):
    in_specs = (
        P(AXES, None),
        P(None, None, AXES, None),
        P(None, AXES, None),
        P(AXES, None),
        P(AXES, None),
        P(AXES, None),
        P(),
        P(),
    )
    out_specs = P(AXES, None)
    return jax.shard_map(local, mesh=mesh, in_specs=in_specs, out_specs=out_specs, check_vma=False)
```

```python
import functools
import heapq

import jax
import jax.numpy as jnp
from jax import lax
from jax.experimental import pallas as pl
from jax.experimental.pallas import tpu as pltpu
from jax.sharding import PartitionSpec as P

AXES = ("dp", "expert", "shard")
ROWS = 8
WIDE = 2048
EXTRA = 128
SLOTS = 8
SLIVER = 32
UNITS = 2 * SLOTS * SLIVER
RING = {"x": 4, "y": 4, "z": 8}
ORDER = (("x", "y", "z"), ("z", "y", "x"), ("z", "x", "y"))
RATE, LATENCY = 45500.0, 1.7
AHEAD = 3.0
GATHER_BONUS = {
    (0, 2, 1): 8.4, (2, 2, 1): -1.3, (1, 0, 1): 3.2, (2, 2, "i2", 0): 9.8, (2, 2, 2): -5.4,
    (0, 2, "i2", 3): 7.1, (2, 2, "i2", 3): 3.1, (2, 1, 1): 1.3, (2, 2, "i2", 2): -0.2, (0, 1, 1): 9.9,
    (1, 0, 3): 10.5, (1, 2, "i2", 0): -2.1, (2, 0): 13.6, (0, 2, 4): 2.1, (1, 1): 12.0,
    (0, 2, "i2", 0): -1.6, (0, 2, 2): 12.4, (1, 2, "i2", 1): -0.8, (0, 0, 2): 13.3, (1, 2, 1): 1.1,
    (1, 2, "i2", 2): -3.7, (1, 2, "i2", 3): -11.9, (0, 2, "i2", 1): 3.8, (0, 2): 9.5, (2, 0, 3): 13.3,
    (1, 2): -12.6, (1, 1, 1): 2.7, (1, 2, 2): -9.8, (1, 0, 4): -6.2, (0, 1, 2): -0.8,
    (1, 0, 2): -10.9, (2, 0, 4): -9.6, (2, 2, "i2", 1): 0.4, (1, 0): 0.1, (0, 2, "i2", 2): 12.3,
    (0, 1): 6.0, (2, 2): -7.3, (2, 1): 11.6,
}
SCATTER_BONUS = {
    (2, 2): -11.4, (0, 1): -5.1, (1, 0, 3): -1.7, (1, 0, 1): 6.8, (2, 2, "i2", 3): 7.5,
    (0, 2, 2): -3.0, (2, 1): -1.0, (1, 2, "i2", 2): -1.4, (1, 2): -0.9, (1, 0, 4): 2.1,
    (0, 1, 2): -1.5, (2, 2, 1): 3.3, (1, 1, 2): -10.2, (0, 2, 1): 3.3, (0, 2, "i2", 1): 8.6,
    (1, 2, "i2", 0): -2.1, (2, 2, "i2", 2): -0.3, (1, 1, 1): -0.2, (2, 0, 2): 0.7, (2, 0, 4): -6.7,
    (2, 0, 3): -6.4, (2, 0, 1): -9.0, (0, 0, 1): 2.7, (1, 2, "i2", 3): 1.5, (2, 0): 11.5,
    (0, 2, 4): -7.1, (0, 0): -12.4, (0, 2, 3): -0.7,
}


class Message:
    def __init__(self, part, stage, dist, sign, sub):
        self.part, self.stage, self.dist, self.sign, self.sub = part, stage, dist, sign, sub
        self.key = (part, stage, dist, sign, sub)
        self.axis = ORDER[part][stage]
        self.link = (self.axis, sign)


def position(ring_index, size):
    r = ring_index % size
    return 0 if r == 0 else (2 * r - 1 if r <= size // 2 else 2 * (size - r))


def groups(n1):
    return [(0, 1), (1, 2), (3, 1)] if n1 == 4 else [(0, 1), (1, 2), (3, 2), (5, 3)]


def subs_of(part, stage):
    n1, n2 = RING[ORDER[part][0]], RING[ORDER[part][1]]
    if stage == 0:
        return [(0, 0, 1)]
    first = [(0, i1, n) for i1, n in groups(n1)]
    if stage == 1:
        return first
    rest = [(0, 4)] if n1 == 4 else [(0, 3), (3, 5)]
    return first + [(i2, i1, n) for i2 in range(1, n2) for i1, n in rest]


def far_sign(part, stage, sub):
    subs = subs_of(part, stage)
    if stage == 0:
        return -1 if part == 2 else 1
    if stage == 1:
        return 1 if sub in (0, len(subs) - 1) else -1
    return 1 if subs[sub][0] in (0, 3) else -1


def messages():
    out = []
    for part in range(3):
        for stage in range(3):
            size = RING[ORDER[part][stage]]
            for dist in range(1, size // 2 + 1):
                for sign in (1, -1):
                    for sub in range(len(subs_of(part, stage))):
                        if dist < size // 2 or far_sign(part, stage, sub) == sign:
                            out.append(Message(part, stage, dist, sign, sub))
    return out


def blocks_of(msg, ring_index):
    i2, i1, n = subs_of(msg.part, msg.stage)[msg.sub]
    p = position(ring_index, RING[msg.axis])
    if msg.stage == 0:
        return [(0, 0, p)]
    if msg.stage == 1:
        return [(0, p, i1 + j) for j in range(n)]
    return [(p, i2, i1 + j) for j in range(n)]


def simulate(sends, recv_needs, jobs, recv_cost, timers=(), ahead=AHEAD, bonus=None):
    readers = {}
    for key, (_, _, needs) in sends.items():
        for token in needs:
            readers.setdefault(token, []).append(key)
    tails = {}

    def tail(key):
        if key not in tails:
            after = max((tail(k) for k in readers.get(("recv",) + key, [])), default=0.0)
            tails[key] = sends[key][1] / RATE + LATENCY + after
        return tails[key]

    number = {key: i for i, key in enumerate(sends)}
    missing = {key: len(needs) for key, (_, _, needs) in sends.items()}
    queues, link_free, arrivals = {}, {}, []
    done, order, ready = set(), [], []
    now = 0.0

    def offer(key):
        part, stage, dist, _, sub = key
        extra = bonus or {}
        i2 = subs_of(part, stage)[sub][0]
        rank = tail(key) + sum(extra.get(k, 0.0) for k in ((part, stage), (part, stage, dist), (part, stage, "i2", i2)))
        heapq.heappush(queues.setdefault(sends[key][0].link, []), (-rank, number[key], key))

    def finish(token):
        done.add(token)
        for key in readers.get(token, []):
            missing[key] -= 1
            if not missing[key]:
                offer(key)

    def issue():
        for link, queue in queues.items():
            while queue and link_free.get(link, 0.0) - now < ahead:
                key = heapq.heappop(queue)[2]
                order.append(("send", key))
                sent = max(now, link_free.get(link, 0.0)) + sends[key][1] / RATE
                link_free[link] = sent
                heapq.heappush(arrivals, (sent + LATENCY, key))

    for key, count in missing.items():
        if not count:
            offer(key)
    jobs, timers = list(jobs), list(timers)
    handled = 0
    issue()
    while handled < len(sends) or jobs:
        while timers and timers[0][0] <= now:
            token = timers.pop(0)[1]
            order.append(("job", token))
            finish(token)
        while arrivals and arrivals[0][0] <= now:
            ready.append(heapq.heappop(arrivals))
        pick = next((r for r in ready if recv_needs[r[1]] <= done), None)
        job = next((j for j in jobs if j[2] <= done), None)
        if pick is not None:
            ready.remove(pick)
            now += recv_cost(sends[pick[1]])
            order.append(("recv", pick[1]))
            finish(("recv",) + pick[1])
            handled += 1
        elif job is not None:
            jobs.remove(job)
            now += job[1]
            order.append(("job", job[0]))
            finish(job[0])
        else:
            times = [a[0] for a in arrivals[:1]] + [t[0] for t in timers[:1]]
            times += [free - ahead + 0.01 for link, free in link_free.items() if queues.get(link)]
            now = max(now, min(times))
        issue()
    return order, now


def gather_order():
    msgs = messages()
    source = {}
    for m in msgs:
        for b in blocks_of(m, -m.dist * m.sign):
            source[(m.part,) + b] = ("recv",) + m.key
    sends = {}
    for m in msgs:
        src = blocks_of(m, -(m.dist - 1) * m.sign)
        needs = {source[(m.part,) + b] for b in src if (m.part,) + b in source}
        width = WIDE + (EXTRA if m.part == 0 else 0)
        sends[m.key] = (m, len(src) * ROWS * width * 2, needs)
    jobs = []
    for part, slabs, i2s, held in GATE_UP_JOBS:
        needs = {v for k, v in source.items() if k[0] == part and k[1] in slabs and k[2] in i2s}
        rows = (32 if part == 0 else 64) * len(i2s) * len(slabs)
        cost = PREPARE_COST * rows + UP_COST[rows] * len(held)
        jobs.append((("up", part, slabs, i2s, held), cost, needs | {("weights", held[-1])}))
    timers = [(OWN_AT, ("weights", 0)), (PARTNER_AT, ("weights", 1))]
    return sends, simulate(sends, {m.key: set() for m in msgs}, jobs, lambda s: 0.05, timers, bonus=GATHER_BONUS)


OWN_AT, PARTNER_AT = 5.0, 20.0
PREPARE_COST = 0.0008
UP_COST = {64: 0.65, 128: 0.67, 192: 0.7, 256: 0.76, 384: 1.08}
HIDDEN_COST = (0.8, 0.4, 0.7, 1.5)
ALL = (0, 1, 2, 3)
GATE_UP_JOBS = (
    (2, (1,), ALL, (0, 1)),
    (1, (0,), ALL, (0, 1)),
    (2, (3,), (0,), (0, 1)),
    (0, (3, 4), ALL, (0, 1)),
    (2, (3,), (1, 2, 3), (0, 1)),
    (0, (7,), ALL, (0, 1)),
    (2, (0,), ALL, (0, 1)),
    (1, (1,), ALL, (0, 1)),
    (0, (5, 6), ALL, (0, 1)),
    (2, (2,), ALL, (0, 1)),
    (0, (0, 1, 2), ALL, (0, 1)),
    (1, (2,), ALL, (0, 1)),
    (1, (3,), ALL, (0, 1)),
)
DOWN_JOBS = (
    ("hid", 0), (2, (3,)), ("hid", 1), (0, (7,)), ("hid", 2), (1, (3,)),
    ("hid", 3), (0, (5, 6)), (1, (1,)), (2, (1,)), (2, (2,)), (0, (3, 4)),
    (1, (2,)), (2, (0,)), (0, (1, 2)), (1, (0,)), (0, (0,)),
)


def scatter_order():
    msgs = messages()[::-1]
    job_of = {}
    for part, slabs in DOWN_JOBS:
        if part != "hid":
            for i3 in slabs:
                job_of[(part, i3)] = ("down", part, slabs)
    adds = {}
    for m in msgs:
        for b in blocks_of(m, (m.dist - 1) * m.sign):
            adds.setdefault((m.part,) + b, []).append(m)
    sends, recv_needs = {}, {}
    for m in msgs:
        src = blocks_of(m, m.dist * m.sign)
        needs = set()
        for b in src:
            needs.add(job_of[(m.part, b[0])])
            for a in adds.get((m.part,) + b, []):
                if a.stage > m.stage or (a.stage == m.stage and a.sign == m.sign and a.dist == m.dist + 1):
                    needs.add(("recv",) + a.key)
        sends[m.key] = (m, len(src) * ROWS * WIDE * 2, needs)
        recv_needs[m.key] = {job_of[(m.part, b[0])] for b in blocks_of(m, (m.dist - 1) * m.sign)}
    jobs = []
    for part, slabs in DOWN_JOBS:
        if part == "hid":
            jobs.append((("hid", slabs), HIDDEN_COST[slabs], set()))
        else:
            jobs.append((("down", part, slabs), 0.75 * len(slabs) if part == 0 else 1.1, set()))
    return sends, simulate(sends, recv_needs, jobs, lambda s: 0.04 + s[1] * 0.8e-6, bonus=SCATTER_BONUS)


def device_at(x, y, z, core):
    x, y, z = lax.rem(x + 4, 4), lax.rem(y + 4, 4), lax.rem(z + 8, 8)
    return (lax.rem(x, 2), z, (x // 2) * 8 + y * 2 + core)


def kernel(
    tok_ref, gu_ref, dn_ref, ids_hbm, gv_hbm, old_hbm, new_hbm, out_ref,
    tok0, tok1, tok2, w_gu, w_dn, acc, scale, spread, xs, hs,
    l30, l20, l10, l31, l21, l11, l32, l22, l12,
    ids_ref, gv_ref, old_ref, new_ref, table_sem, own_sem, w_send, w_recv, ag_send, ag_recv, rs_send, rs_recv,
):
    toks = (tok0, tok1, tok2)
    lands = ((l10, l20, l30), (l11, l21, l31), (l12, l22, l32))
    dp, z, shard = (lax.axis_index(a) for a in AXES)
    core, y, x = lax.rem(shard, 2), lax.rem(shard // 2, 4), (shard // 8) * 2 + dp
    partner = device_at(x, y, z, 1 - core)
    near = {
        ("x", 1): device_at(x + 1, y, z, core), ("x", -1): device_at(x - 1, y, z, core),
        ("y", 1): device_at(x, y + 1, z, core), ("y", -1): device_at(x, y - 1, z, core),
        ("z", 1): device_at(x, y, z + 1, core), ("z", -1): device_at(x, y, z - 1, core),
    }
    mesh_id = pl.DeviceIdType.MESH
    barrier = pltpu.get_barrier_semaphore()
    for dev in (partner, *near.values()):
        pl.semaphore_signal(barrier, inc=1, device_id=dev, device_id_type=mesh_id)

    tables = [
        pltpu.make_async_copy(src, dst, table_sem.at[i])
        for i, (src, dst) in enumerate(((ids_hbm, ids_ref), (gv_hbm, gv_ref), (old_hbm, old_ref), (new_hbm, new_ref)))
    ]
    for copy in tables:
        copy.start()
    own = [
        pltpu.make_async_copy(tok_ref.at[:, pl.ds(p * WIDE, WIDE)], toks[p].at[0, 0, 0, :, pl.ds(0, WIDE)], own_sem.at[p])
        for p in range(3)
    ]
    for copy in own:
        copy.start()
    own_w = [
        pltpu.make_async_copy(gu_ref.at[:, 0], w_gu.at[0, 0], own_sem.at[3]),
        pltpu.make_async_copy(gu_ref.at[:, 1], w_gu.at[0, 1], own_sem.at[4]),
        pltpu.make_async_copy(dn_ref, w_dn.at[0], own_sem.at[5]),
    ]
    for copy in own_w:
        copy.start()

    for copy in tables:
        copy.wait()

    lane = lax.broadcasted_iota(jnp.int32, (ROWS, EXTRA), 1)
    slot = lax.rem(lane, SLOTS)
    diagonal = lax.broadcasted_iota(jnp.int32, (ROWS, ROWS), 0) == lax.broadcasted_iota(jnp.int32, (ROWS, ROWS), 1)

    def column(ref, k):
        row = jnp.broadcast_to(ref[k : k + 1, :], (ROWS, ROWS))
        return jnp.sum(jnp.where(diagonal, row, jnp.zeros_like(row)), axis=1, keepdims=True)

    held = jnp.zeros((ROWS, EXTRA), jnp.int32)
    for j in range(SLOTS):
        held = jnp.where(slot == j, old_ref[j], held)
    weight = jnp.zeros((ROWS, EXTRA), jnp.float32)
    for k in range(2):
        ids = jnp.broadcast_to(column(ids_ref, k), (ROWS, EXTRA))
        gate = jnp.broadcast_to(column(gv_ref, k), (ROWS, EXTRA))
        place = jnp.zeros((ROWS, EXTRA), jnp.int32)
        for e in range(SLOTS):
            place = jnp.where(ids == e, new_ref[e], place)
        weight = weight + jnp.where(place == held, gate, 0.0)
    high = weight.astype(jnp.bfloat16).astype(jnp.float32)
    coded = jnp.where(lane < SLOTS, high, jnp.where(lane < 2 * SLOTS, weight - high, 0.0))
    tok0[0, 0, 0, :, WIDE:] = coded.astype(jnp.bfloat16)

    own[0].wait()
    pl.semaphore_wait(barrier, 7)

    def remote(src, dst, send, recv, dev):
        return pltpu.make_async_remote_copy(
            src_ref=src, dst_ref=dst, send_sem=send, recv_sem=recv, device_id=dev, device_id_type=mesh_id
        )

    def view(msg, ring_index, narrow):
        i3, i2, i1 = blocks_of(msg, ring_index)[0]
        n = subs_of(msg.part, msg.stage)[msg.sub][2]
        ref = toks[msg.part]
        if narrow and msg.part == 0:
            return ref.at[i3, i2, pl.ds(i1, n), :, pl.ds(0, WIDE)]
        return ref.at[i3, i2, pl.ds(i1, n)]

    ag_sends, (ag_order, _) = gather_order()
    index = {key: i for i, key in enumerate(ag_sends)}
    gathers = {}
    for key, (m, _, _) in ag_sends.items():
        source, target = view(m, -(m.dist - 1) * m.sign, False), view(m, -m.dist * m.sign, False)
        if m.part and blocks_of(m, -(m.dist - 1) * m.sign) == [(0, 0, 0)]:
            source, target = tok_ref.at[:, pl.ds(m.part * WIDE, WIDE)], target.at[0]
        gathers[key] = remote(
            source, target,
            ag_send.at[index[key]], ag_recv.at[index[key]], near[m.link],
        )
    crossing = [
        remote(gu_ref.at[:, 0], w_gu.at[1, 0], w_send.at[0], w_recv.at[0], partner),
        remote(gu_ref.at[:, 1], w_gu.at[1, 1], w_send.at[1], w_recv.at[1], partner),
        remote(dn_ref, w_dn.at[1], w_send.at[2], w_recv.at[2], partner),
    ]

    def gate_up(part, slabs, i2s, held):
        ref = toks[part]
        count, rows = len(i2s), ref.shape[2] * ROWS
        step = i2s[1] - i2s[0] if count > 1 else 1
        for j, i3 in enumerate(slabs):

            @pl.loop(0, count)
            def _(i2):
                block = ref[i3, i2s[0] + step * i2, :, :, pl.ds(0, WIDE)].astype(jnp.float32)
                start = pl.multiple_of((j * count + i2) * rows, 16)
                xs[pl.ds(start, rows), :] = block.reshape(rows, WIDE).astype(jnp.bfloat16)

        total = count * rows * len(slabs)

        @pl.loop(held[0], held[-1] + 1)
        def _(group):
            right = w_gu[group, :, :, :, pl.ds(part * WIDE, WIDE)].reshape(UNITS, WIDE)
            prod = lax.dot_general(
                xs[0:total, :], right, (((1,), (1,)), ((), ())), preferred_element_type=jnp.float32
            )
            cols = pl.ds(pl.multiple_of(group * UNITS, UNITS), UNITS)
            if part == 0:
                for j, i3 in enumerate(slabs):
                    acc[i3, :, :, :, cols] += prod[j * 128 : (j + 1) * 128].reshape(4, 4, ROWS, UNITS)
            else:
                for i2 in range(count):
                    where = (i2s[i2], slabs[0]) if part == 1 else (slabs[0], i2s[i2])
                    acc[:, where[0], where[1], :, cols] += prod[i2 * 64 : (i2 + 1) * 64].reshape(8, ROWS, UNITS)

        if part == 0 and held[-1] == 1:
            for i3 in slabs:
                code = tok0[i3, :, :, :, pl.ds(WIDE, EXTRA)].astype(jnp.float32).reshape(128, EXTRA)
                wide = jnp.dot(code.astype(jnp.bfloat16), spread[...], preferred_element_type=jnp.float32)
                scale[i3] = wide.reshape(4, 4, ROWS, UNITS)

    crossed = False
    for kind, what in ag_order:
        if kind != "send" and not crossed:
            crossed = True
            for copy in crossing:
                copy.start()
            acc[...] = jnp.zeros_like(acc)
            code_row = lax.broadcasted_iota(jnp.int32, (EXTRA, UNITS), 0)
            unit_slot = lax.rem(lax.broadcasted_iota(jnp.int32, (EXTRA, UNITS), 1) // SLIVER, SLOTS)
            chosen = (code_row < 2 * SLOTS) & (lax.rem(code_row, SLOTS) == unit_slot)
            spread[...] = jnp.where(chosen, 1.0, 0.0).astype(jnp.bfloat16)
        if kind == "send":
            gathers[what].start()
        elif kind == "recv":
            gathers[what].wait_recv()
        elif what == ("weights", 1):
            for copy in crossing:
                copy.wait()
        elif what == ("weights", 0):
            for copy in own[1:] + own_w:
                copy.wait()
        else:
            gate_up(*what[1:])
    for copy in gathers.values():
        copy.wait_send()

    def hidden(where):
        width = UNITS // 2
        values = []
        for group in range(2):
            gate = acc[(*where, slice(None), pl.ds(group * UNITS, width))]
            up = acc[(*where, slice(None), pl.ds(group * UNITS + width, width))]
            share = scale[(*where, slice(None), pl.ds(group * width, width))]
            values.append(gate / (1.0 + jnp.exp(-gate)) * up * share)
        for group in range(2):
            acc[(*where, slice(None), pl.ds(group * width, width))] = values[group]

    def hidden_rows(step):
        if step == 0:
            pl.loop(0, 8)(lambda i: hidden((i, 3, slice(None))))
        elif step == 1:
            pl.loop(0, 3)(lambda i: hidden((7, i, slice(None))))
        elif step == 2:
            pl.loop(0, 7)(lambda i: hidden((i, pl.ds(0, 3), 3)))
        else:
            pl.loop(0, 21)(lambda i: hidden((i // 3, lax.rem(i, 3), pl.ds(0, 3))))

    def down(part, slabs):
        total = 128 * len(slabs) if part == 0 else 256
        if part == 0:
            for j, i3 in enumerate(slabs):
                hs[j * 128 : (j + 1) * 128, :] = acc[i3, :, :, :, pl.ds(0, UNITS)].reshape(128, UNITS).astype(jnp.bfloat16)
        else:
            for i2 in range(4):
                where = (i2, slabs[0]) if part == 1 else (slabs[0], i2)
                rows = acc[:, where[0], where[1], :, pl.ds(0, UNITS)].reshape(64, UNITS)
                hs[i2 * 64 : (i2 + 1) * 64, :] = rows.astype(jnp.bfloat16)

        @pl.loop(0, WIDE // 512)
        def _(n):
            cols = pl.ds(pl.multiple_of(part * WIDE + n * 512, 512), 512)
            right = w_dn[:, :, :, cols].reshape(UNITS, 512)
            prod = jnp.dot(hs[0:total, :], right, preferred_element_type=jnp.float32)
            cols = pl.ds(pl.multiple_of(n * 512, 512), 512)
            ref = toks[part]
            n2, n1 = ref.shape[1], ref.shape[2]
            for j, i3 in enumerate(slabs):
                piece = prod[j * 128 : (j + 1) * 128] if part == 0 else prod
                ref[i3, :, :, :, cols] = piece.reshape(n2, n1, ROWS, 512).astype(jnp.bfloat16)

    rs_sends, (rs_order, _) = scatter_order()

    def landing(m):
        i2, i1, n = subs_of(m.part, m.stage)[m.sub]
        return lands[m.part][m.stage].at[0 if m.sign == 1 else 1, m.dist - 1, i2, pl.ds(i1, n)]

    scatters = {}
    for key, (m, _, _) in rs_sends.items():
        scatters[key] = remote(
            view(m, m.dist * m.sign, True), landing(m),
            rs_send.at[index[key]], rs_recv.at[index[key]], near[m.link],
        )
    for kind, what in rs_order:
        if kind == "send":
            scatters[what].start()
        elif kind == "job" and what[0] == "hid":
            hidden_rows(what[1])
        elif kind == "job":
            down(what[1], what[2])
        else:
            m = rs_sends[what][0]
            scatters[what].wait_recv()
            target = view(m, (m.dist - 1) * m.sign, True)
            target[...] = target[...] + landing(m)[...]
    for p in range(3):
        out_ref[:, p * WIDE : (p + 1) * WIDE] = toks[p][0, 0, 0, :, 0:WIDE]
    for copy in scatters.values():
        copy.wait_send()


def local(
    tokens, gate_up_weight, down_weight, expert_ids, slot_ids, gate_values, old_place, new_place
):
    count = len(messages())
    bf16, f32 = jnp.bfloat16, jnp.float32
    any_space = pl.BlockSpec(memory_space=pl.ANY)
    vmem = pl.BlockSpec(memory_space=pltpu.VMEM)
    lands = []
    for part in range(3):
        for stage in (2, 1, 0):
            n1, n2, _ = (RING[axis] for axis in ORDER[part])
            ring = RING[ORDER[part][stage]]
            shape = (n2 if stage == 2 else 1, n1 if stage else 1)
            lands.append(pltpu.VMEM((2, ring // 2, *shape, ROWS, WIDE), bf16))
    return pl.pallas_call(
        kernel,
        out_shape=jax.ShapeDtypeStruct((ROWS, 3 * WIDE), bf16),
        in_specs=[any_space] * 7,
        out_specs=vmem,
        scratch_shapes=[
            pltpu.VMEM((8, 4, 4, ROWS, WIDE + EXTRA), bf16),
            pltpu.VMEM((4, 4, 8, ROWS, WIDE), bf16),
            pltpu.VMEM((4, 4, 8, ROWS, WIDE), bf16),
            pltpu.VMEM((2, 2, SLOTS, SLIVER, 3 * WIDE), bf16),
            pltpu.VMEM((2, SLOTS, SLIVER, 3 * WIDE), bf16),
            pltpu.VMEM((8, 4, 4, ROWS, 2 * UNITS), f32),
            pltpu.VMEM((8, 4, 4, ROWS, UNITS), f32),
            pltpu.VMEM((EXTRA, UNITS), bf16),
            pltpu.VMEM((384, WIDE), bf16),
            pltpu.VMEM((256, UNITS), bf16),
            *lands,
            pltpu.VMEM((2, ROWS), jnp.int32),
            pltpu.VMEM((2, ROWS), f32),
            pltpu.SMEM((SLOTS,), jnp.int32),
            pltpu.SMEM((SLOTS,), jnp.int32),
            pltpu.SemaphoreType.DMA((4,)),
            pltpu.SemaphoreType.DMA((6,)),
            pltpu.SemaphoreType.DMA((3,)),
            pltpu.SemaphoreType.DMA((3,)),
            pltpu.SemaphoreType.DMA((count,)),
            pltpu.SemaphoreType.DMA((count,)),
            pltpu.SemaphoreType.DMA((count,)),
            pltpu.SemaphoreType.DMA((count,)),
        ],
        compiler_params=pltpu.CompilerParams(
            collective_id=0, has_side_effects=True, vmem_limit_bytes=67043328
        ),
        name="expert_layer",
    )(tokens, gate_up_weight, down_weight, expert_ids.T, gate_values.T, old_place, new_place)


def solution(mesh):
    in_specs = (
        P(AXES, None),
        P(None, None, AXES, None),
        P(None, AXES, None),
        P(AXES, None),
        P(AXES, None),
        P(AXES, None),
        P(),
        P(),
    )
    out_specs = P(AXES, None)
    return jax.shard_map(local, mesh=mesh, in_specs=in_specs, out_specs=out_specs, check_vma=False)
```

```python
import functools
import heapq

import jax
import jax.numpy as jnp
from jax import lax
from jax.experimental import pallas as pl
from jax.experimental.pallas import tpu as pltpu
from jax.sharding import PartitionSpec as P

AXES = ("dp", "expert", "shard")
ROWS = 8
WIDE = 2048
EXTRA = 128
SLOTS = 8
SLIVER = 32
UNITS = 2 * SLOTS * SLIVER
RING = {"x": 4, "y": 4, "z": 8}
ORDER = (("x", "y", "z"), ("z", "y", "x"), ("z", "x", "y"))
RATE, LATENCY = 45500.0, 1.7
AHEAD = 3.0
GATHER_BONUS = {
    (0, 2, 1): 8.4, (2, 2, 1): -1.3, (1, 0, 1): 3.2, (2, 2, "i2", 0): 9.8, (2, 2, 2): -5.4,
    (0, 2, "i2", 3): 7.1, (2, 2, "i2", 3): 3.1, (2, 1, 1): 1.3, (2, 2, "i2", 2): -0.2, (0, 1, 1): 9.9,
    (1, 0, 3): 10.5, (1, 2, "i2", 0): -2.1, (2, 0): 13.6, (0, 2, 4): 2.1, (1, 1): 12.0,
    (0, 2, "i2", 0): -1.6, (0, 2, 2): 12.4, (1, 2, "i2", 1): -0.8, (0, 0, 2): 13.3, (1, 2, 1): 1.1,
    (1, 2, "i2", 2): -3.7, (1, 2, "i2", 3): -11.9, (0, 2, "i2", 1): 3.8, (0, 2): 9.5, (2, 0, 3): 13.3,
    (1, 2): -12.6, (1, 1, 1): 2.7, (1, 2, 2): -9.8, (1, 0, 4): -6.2, (0, 1, 2): -0.8,
    (1, 0, 2): -10.9, (2, 0, 4): -9.6, (2, 2, "i2", 1): 0.4, (1, 0): 0.1, (0, 2, "i2", 2): 12.3,
    (0, 1): 6.0, (2, 2): -7.3, (2, 1): 11.6,
}
SCATTER_BONUS = {
    (2, 2): -11.4, (0, 1): -5.1, (1, 0, 3): -1.7, (1, 0, 1): 6.8, (2, 2, "i2", 3): 7.5,
    (0, 2, 2): -3.0, (2, 1): -1.0, (1, 2, "i2", 2): -1.4, (1, 2): -0.9, (1, 0, 4): 2.1,
    (0, 1, 2): -1.5, (2, 2, 1): 3.3, (1, 1, 2): -10.2, (0, 2, 1): 3.3, (0, 2, "i2", 1): 8.6,
    (1, 2, "i2", 0): -2.1, (2, 2, "i2", 2): -0.3, (1, 1, 1): -0.2, (2, 0, 2): 0.7, (2, 0, 4): -6.7,
    (2, 0, 3): -6.4, (2, 0, 1): -9.0, (0, 0, 1): 2.7, (1, 2, "i2", 3): 1.5, (2, 0): 11.5,
    (0, 2, 4): -7.1, (0, 0): -12.4, (0, 2, 3): -0.7,
}


class Message:
    def __init__(self, part, stage, dist, sign, sub):
        self.part, self.stage, self.dist, self.sign, self.sub = part, stage, dist, sign, sub
        self.key = (part, stage, dist, sign, sub)
        self.axis = ORDER[part][stage]
        self.link = (self.axis, sign)


def position(ring_index, size):
    r = ring_index % size
    return 0 if r == 0 else (2 * r - 1 if r <= size // 2 else 2 * (size - r))


def groups(n1):
    return [(0, 1), (1, 2), (3, 1)] if n1 == 4 else [(0, 1), (1, 2), (3, 2), (5, 3)]


def subs_of(part, stage):
    n1, n2 = RING[ORDER[part][0]], RING[ORDER[part][1]]
    if stage == 0:
        return [(0, 0, 1)]
    first = [(0, i1, n) for i1, n in groups(n1)]
    if stage == 1:
        return first
    rest = [(0, 4)] if n1 == 4 else [(0, 3), (3, 5)]
    return first + [(i2, i1, n) for i2 in range(1, n2) for i1, n in rest]


def far_sign(part, stage, sub):
    subs = subs_of(part, stage)
    if stage == 0:
        return -1 if part == 2 else 1
    if stage == 1:
        return 1 if sub in (0, len(subs) - 1) else -1
    return 1 if subs[sub][0] in (0, 3) else -1


def messages():
    out = []
    for part in range(3):
        for stage in range(3):
            size = RING[ORDER[part][stage]]
            for dist in range(1, size // 2 + 1):
                for sign in (1, -1):
                    for sub in range(len(subs_of(part, stage))):
                        if dist < size // 2 or far_sign(part, stage, sub) == sign:
                            out.append(Message(part, stage, dist, sign, sub))
    return out


def blocks_of(msg, ring_index):
    i2, i1, n = subs_of(msg.part, msg.stage)[msg.sub]
    p = position(ring_index, RING[msg.axis])
    if msg.stage == 0:
        return [(0, 0, p)]
    if msg.stage == 1:
        return [(0, p, i1 + j) for j in range(n)]
    return [(p, i2, i1 + j) for j in range(n)]


def simulate(sends, recv_needs, jobs, recv_cost, timers=(), ahead=AHEAD, bonus=None):
    readers = {}
    for key, (_, _, needs) in sends.items():
        for token in needs:
            readers.setdefault(token, []).append(key)
    tails = {}

    def tail(key):
        if key not in tails:
            after = max((tail(k) for k in readers.get(("recv",) + key, [])), default=0.0)
            tails[key] = sends[key][1] / RATE + LATENCY + after
        return tails[key]

    number = {key: i for i, key in enumerate(sends)}
    missing = {key: len(needs) for key, (_, _, needs) in sends.items()}
    queues, link_free, arrivals = {}, {}, []
    done, order, ready = set(), [], []
    now = 0.0

    def offer(key):
        part, stage, dist, _, sub = key
        extra = bonus or {}
        i2 = subs_of(part, stage)[sub][0]
        rank = tail(key) + sum(extra.get(k, 0.0) for k in ((part, stage), (part, stage, dist), (part, stage, "i2", i2)))
        heapq.heappush(queues.setdefault(sends[key][0].link, []), (-rank, number[key], key))

    def finish(token):
        done.add(token)
        for key in readers.get(token, []):
            missing[key] -= 1
            if not missing[key]:
                offer(key)

    def issue():
        for link, queue in queues.items():
            while queue and link_free.get(link, 0.0) - now < ahead:
                key = heapq.heappop(queue)[2]
                order.append(("send", key))
                sent = max(now, link_free.get(link, 0.0)) + sends[key][1] / RATE
                link_free[link] = sent
                heapq.heappush(arrivals, (sent + LATENCY, key))

    for key, count in missing.items():
        if not count:
            offer(key)
    jobs, timers = list(jobs), list(timers)
    handled = 0
    issue()
    while handled < len(sends) or jobs:
        while timers and timers[0][0] <= now:
            token = timers.pop(0)[1]
            order.append(("job", token))
            finish(token)
        while arrivals and arrivals[0][0] <= now:
            ready.append(heapq.heappop(arrivals))
        pick = next((r for r in ready if recv_needs[r[1]] <= done), None)
        job = next((j for j in jobs if j[2] <= done), None)
        if pick is not None:
            ready.remove(pick)
            now += recv_cost(sends[pick[1]])
            order.append(("recv", pick[1]))
            finish(("recv",) + pick[1])
            handled += 1
        elif job is not None:
            jobs.remove(job)
            now += job[1]
            order.append(("job", job[0]))
            finish(job[0])
        else:
            times = [a[0] for a in arrivals[:1]] + [t[0] for t in timers[:1]]
            times += [free - ahead + 0.01 for link, free in link_free.items() if queues.get(link)]
            now = max(now, min(times))
        issue()
    return order, now


def gather_order():
    msgs = messages()
    source = {}
    for m in msgs:
        for b in blocks_of(m, -m.dist * m.sign):
            source[(m.part,) + b] = ("recv",) + m.key
    sends = {}
    for m in msgs:
        src = blocks_of(m, -(m.dist - 1) * m.sign)
        needs = {source[(m.part,) + b] for b in src if (m.part,) + b in source}
        width = WIDE + (EXTRA if m.part == 0 else 0)
        sends[m.key] = (m, len(src) * ROWS * width * 2, needs)
    jobs = []
    for part, slabs, i2s, held in GATE_UP_JOBS:
        needs = {v for k, v in source.items() if k[0] == part and k[1] in slabs and k[2] in i2s}
        rows = (32 if part == 0 else 64) * len(i2s) * len(slabs)
        cost = PREPARE_COST * rows + UP_COST[rows] * len(held)
        jobs.append((("up", part, slabs, i2s, held), cost, needs | {("weights", held[-1])}))
    timers = [(OWN_AT, ("weights", 0)), (PARTNER_AT, ("weights", 1))]
    return sends, simulate(sends, {m.key: set() for m in msgs}, jobs, lambda s: 0.05, timers, bonus=GATHER_BONUS)


OWN_AT, PARTNER_AT = 5.0, 20.0
PREPARE_COST = 0.0001
UP_COST = {64: 0.65, 128: 0.67, 192: 0.7, 256: 0.76, 384: 1.08}
HIDDEN_COST = (0.8, 0.4, 0.7, 1.5)
ALL = (0, 1, 2, 3)
GATE_UP_JOBS = (
    (2, (1,), ALL, (0, 1)),
    (1, (0,), ALL, (0, 1)),
    (2, (3,), (0,), (0, 1)),
    (0, (3, 4), ALL, (0, 1)),
    (2, (3,), (1, 2, 3), (0, 1)),
    (0, (7,), ALL, (0, 1)),
    (2, (0,), ALL, (0, 1)),
    (1, (1,), ALL, (0, 1)),
    (0, (5, 6), ALL, (0, 1)),
    (2, (2,), ALL, (0, 1)),
    (0, (0, 1, 2), ALL, (0, 1)),
    (1, (2,), ALL, (0, 1)),
    (1, (3,), ALL, (0, 1)),
)
DOWN_JOBS = (
    ("hid", 0), (2, (3,)), ("hid", 1), (0, (7,)), ("hid", 2), (1, (3,)),
    ("hid", 3), (0, (5, 6)), (1, (1,)), (2, (1,)), (2, (2,)), (0, (3, 4)),
    (1, (2,)), (2, (0,)), (0, (1, 2)), (1, (0,)), (0, (0,)),
)


def scatter_order():
    msgs = messages()[::-1]
    job_of = {}
    for part, slabs in DOWN_JOBS:
        if part != "hid":
            for i3 in slabs:
                job_of[(part, i3)] = ("down", part, slabs)
    adds = {}
    for m in msgs:
        for b in blocks_of(m, (m.dist - 1) * m.sign):
            adds.setdefault((m.part,) + b, []).append(m)
    sends, recv_needs = {}, {}
    for m in msgs:
        src = blocks_of(m, m.dist * m.sign)
        needs = set()
        for b in src:
            needs.add(job_of[(m.part, b[0])])
            for a in adds.get((m.part,) + b, []):
                if a.stage > m.stage or (a.stage == m.stage and a.sign == m.sign and a.dist == m.dist + 1):
                    needs.add(("recv",) + a.key)
        sends[m.key] = (m, len(src) * ROWS * WIDE * 2, needs)
        recv_needs[m.key] = {job_of[(m.part, b[0])] for b in blocks_of(m, (m.dist - 1) * m.sign)}
    jobs = []
    for part, slabs in DOWN_JOBS:
        if part == "hid":
            jobs.append((("hid", slabs), HIDDEN_COST[slabs], set()))
        else:
            jobs.append((("down", part, slabs), 0.75 * len(slabs) if part == 0 else 1.1, set()))
    return sends, simulate(sends, recv_needs, jobs, lambda s: 0.04 + s[1] * 0.8e-6, bonus=SCATTER_BONUS)


def device_at(x, y, z, core):
    x, y, z = lax.rem(x + 4, 4), lax.rem(y + 4, 4), lax.rem(z + 8, 8)
    return (lax.rem(x, 2), z, (x // 2) * 8 + y * 2 + core)


def kernel(
    tok_ref, gu_ref, dn_ref, ids_hbm, gv_hbm, old_hbm, new_hbm, out_ref,
    tok0, tok1, tok2, w_gu, w_dn, acc, scale, spread, hs,
    l30, l20, l10, l31, l21, l11, l32, l22, l12,
    ids_ref, gv_ref, old_ref, new_ref, table_sem, own_sem, w_send, w_recv, ag_send, ag_recv, rs_send, rs_recv,
):
    toks = (tok0, tok1, tok2)
    lands = ((l10, l20, l30), (l11, l21, l31), (l12, l22, l32))
    dp, z, shard = (lax.axis_index(a) for a in AXES)
    core, y, x = lax.rem(shard, 2), lax.rem(shard // 2, 4), (shard // 8) * 2 + dp
    partner = device_at(x, y, z, 1 - core)
    near = {
        ("x", 1): device_at(x + 1, y, z, core), ("x", -1): device_at(x - 1, y, z, core),
        ("y", 1): device_at(x, y + 1, z, core), ("y", -1): device_at(x, y - 1, z, core),
        ("z", 1): device_at(x, y, z + 1, core), ("z", -1): device_at(x, y, z - 1, core),
    }
    mesh_id = pl.DeviceIdType.MESH
    barrier = pltpu.get_barrier_semaphore()
    for dev in (partner, *near.values()):
        pl.semaphore_signal(barrier, inc=1, device_id=dev, device_id_type=mesh_id)

    tables = [
        pltpu.make_async_copy(src, dst, table_sem.at[i])
        for i, (src, dst) in enumerate(((ids_hbm, ids_ref), (gv_hbm, gv_ref), (old_hbm, old_ref), (new_hbm, new_ref)))
    ]
    for copy in tables:
        copy.start()
    own = [
        pltpu.make_async_copy(tok_ref.at[:, pl.ds(p * WIDE, WIDE)], toks[p].at[0, 0, 0, :, pl.ds(0, WIDE)], own_sem.at[p])
        for p in range(3)
    ]
    for copy in own:
        copy.start()
    own_w = [
        pltpu.make_async_copy(gu_ref.at[:, 0], w_gu.at[0, 0], own_sem.at[3]),
        pltpu.make_async_copy(gu_ref.at[:, 1], w_gu.at[0, 1], own_sem.at[4]),
        pltpu.make_async_copy(dn_ref, w_dn.at[0], own_sem.at[5]),
    ]
    for copy in own_w:
        copy.start()

    for copy in tables:
        copy.wait()

    lane = lax.broadcasted_iota(jnp.int32, (ROWS, EXTRA), 1)
    slot = lax.rem(lane, SLOTS)
    diagonal = lax.broadcasted_iota(jnp.int32, (ROWS, ROWS), 0) == lax.broadcasted_iota(jnp.int32, (ROWS, ROWS), 1)

    def column(ref, k):
        row = jnp.broadcast_to(ref[k : k + 1, :], (ROWS, ROWS))
        return jnp.sum(jnp.where(diagonal, row, jnp.zeros_like(row)), axis=1, keepdims=True)

    held = jnp.zeros((ROWS, EXTRA), jnp.int32)
    for j in range(SLOTS):
        held = jnp.where(slot == j, old_ref[j], held)
    weight = jnp.zeros((ROWS, EXTRA), jnp.float32)
    for k in range(2):
        ids = jnp.broadcast_to(column(ids_ref, k), (ROWS, EXTRA))
        gate = jnp.broadcast_to(column(gv_ref, k), (ROWS, EXTRA))
        place = jnp.zeros((ROWS, EXTRA), jnp.int32)
        for e in range(SLOTS):
            place = jnp.where(ids == e, new_ref[e], place)
        weight = weight + jnp.where(place == held, gate, 0.0)
    high = weight.astype(jnp.bfloat16).astype(jnp.float32)
    coded = jnp.where(lane < SLOTS, high, jnp.where(lane < 2 * SLOTS, weight - high, 0.0))
    tok0[0, 0, 0, :, WIDE:] = coded.astype(jnp.bfloat16)

    own[0].wait()
    pl.semaphore_wait(barrier, 7)

    def remote(src, dst, send, recv, dev):
        return pltpu.make_async_remote_copy(
            src_ref=src, dst_ref=dst, send_sem=send, recv_sem=recv, device_id=dev, device_id_type=mesh_id
        )

    def view(msg, ring_index, narrow):
        i3, i2, i1 = blocks_of(msg, ring_index)[0]
        n = subs_of(msg.part, msg.stage)[msg.sub][2]
        ref = toks[msg.part]
        if narrow and msg.part == 0:
            return ref.at[i3, i2, pl.ds(i1, n), :, pl.ds(0, WIDE)]
        return ref.at[i3, i2, pl.ds(i1, n)]

    ag_sends, (ag_order, _) = gather_order()
    index = {key: i for i, key in enumerate(ag_sends)}
    gathers = {}
    for key, (m, _, _) in ag_sends.items():
        source, target = view(m, -(m.dist - 1) * m.sign, False), view(m, -m.dist * m.sign, False)
        if m.part and blocks_of(m, -(m.dist - 1) * m.sign) == [(0, 0, 0)]:
            source, target = tok_ref.at[:, pl.ds(m.part * WIDE, WIDE)], target.at[0]
        gathers[key] = remote(
            source, target,
            ag_send.at[index[key]], ag_recv.at[index[key]], near[m.link],
        )
    crossing = [
        remote(gu_ref.at[:, 0], w_gu.at[1, 0], w_send.at[0], w_recv.at[0], partner),
        remote(gu_ref.at[:, 1], w_gu.at[1, 1], w_send.at[1], w_recv.at[1], partner),
        remote(dn_ref, w_dn.at[1], w_send.at[2], w_recv.at[2], partner),
    ]

    def gate_up(part, slabs, i2s, held):
        ref = toks[part]
        count = len(i2s)
        total = len(slabs) * count * ref.shape[2] * ROWS

        @pl.loop(held[0], held[-1] + 1)
        def _(group):
            right = w_gu[group, :, :, :, pl.ds(part * WIDE, WIDE)].reshape(UNITS, WIDE)
            left = ref[pl.ds(slabs[0], len(slabs)), pl.ds(i2s[0], count), :, :, pl.ds(0, WIDE)].reshape(total, WIDE)
            prod = lax.dot_general(
                left, right, (((1,), (1,)), ((), ())), preferred_element_type=jnp.float32
            )
            cols = pl.ds(pl.multiple_of(group * UNITS, UNITS), UNITS)
            if part == 0:
                for j, i3 in enumerate(slabs):
                    acc[i3, :, :, :, cols] += prod[j * 128 : (j + 1) * 128].reshape(4, 4, ROWS, UNITS)
            else:
                for i2 in range(count):
                    where = (i2s[i2], slabs[0]) if part == 1 else (slabs[0], i2s[i2])
                    acc[:, where[0], where[1], :, cols] += prod[i2 * 64 : (i2 + 1) * 64].reshape(8, ROWS, UNITS)

        if part == 0 and held[-1] == 1:
            for i3 in slabs:
                code = tok0[i3, :, :, :, pl.ds(WIDE, EXTRA)].astype(jnp.float32).reshape(128, EXTRA)
                wide = jnp.dot(code.astype(jnp.bfloat16), spread[...], preferred_element_type=jnp.float32)
                scale[i3] = wide.reshape(4, 4, ROWS, UNITS)

    crossed = False
    for kind, what in ag_order:
        if kind != "send" and not crossed:
            crossed = True
            for copy in crossing:
                copy.start()
            acc[...] = jnp.zeros_like(acc)
            code_row = lax.broadcasted_iota(jnp.int32, (EXTRA, UNITS), 0)
            unit_slot = lax.rem(lax.broadcasted_iota(jnp.int32, (EXTRA, UNITS), 1) // SLIVER, SLOTS)
            chosen = (code_row < 2 * SLOTS) & (lax.rem(code_row, SLOTS) == unit_slot)
            spread[...] = jnp.where(chosen, 1.0, 0.0).astype(jnp.bfloat16)
        if kind == "send":
            gathers[what].start()
        elif kind == "recv":
            gathers[what].wait_recv()
        elif what == ("weights", 1):
            for copy in crossing:
                copy.wait()
        elif what == ("weights", 0):
            for copy in own[1:] + own_w:
                copy.wait()
        else:
            gate_up(*what[1:])
    for copy in gathers.values():
        copy.wait_send()

    def hidden(where):
        width = UNITS // 2
        values = []
        for group in range(2):
            gate = acc[(*where, slice(None), pl.ds(group * UNITS, width))]
            up = acc[(*where, slice(None), pl.ds(group * UNITS + width, width))]
            share = scale[(*where, slice(None), pl.ds(group * width, width))]
            values.append(gate / (1.0 + jnp.exp(-gate)) * up * share)
        for group in range(2):
            acc[(*where, slice(None), pl.ds(group * width, width))] = values[group]

    def hidden_rows(step):
        if step == 0:
            pl.loop(0, 8)(lambda i: hidden((i, 3, slice(None))))
        elif step == 1:
            pl.loop(0, 3)(lambda i: hidden((7, i, slice(None))))
        elif step == 2:
            pl.loop(0, 7)(lambda i: hidden((i, pl.ds(0, 3), 3)))
        else:
            pl.loop(0, 21)(lambda i: hidden((i // 3, lax.rem(i, 3), pl.ds(0, 3))))

    def down(part, slabs):
        total = 128 * len(slabs) if part == 0 else 256
        if part == 0:
            for j, i3 in enumerate(slabs):
                hs[j * 128 : (j + 1) * 128, :] = acc[i3, :, :, :, pl.ds(0, UNITS)].reshape(128, UNITS).astype(jnp.bfloat16)
        else:
            for i2 in range(4):
                where = (i2, slabs[0]) if part == 1 else (slabs[0], i2)
                rows = acc[:, where[0], where[1], :, pl.ds(0, UNITS)].reshape(64, UNITS)
                hs[i2 * 64 : (i2 + 1) * 64, :] = rows.astype(jnp.bfloat16)

        @pl.loop(0, WIDE // 512)
        def _(n):
            cols = pl.ds(pl.multiple_of(part * WIDE + n * 512, 512), 512)
            right = w_dn[:, :, :, cols].reshape(UNITS, 512)
            prod = jnp.dot(hs[0:total, :], right, preferred_element_type=jnp.float32)
            cols = pl.ds(pl.multiple_of(n * 512, 512), 512)
            ref = toks[part]
            n2, n1 = ref.shape[1], ref.shape[2]
            for j, i3 in enumerate(slabs):
                piece = prod[j * 128 : (j + 1) * 128] if part == 0 else prod
                ref[i3, :, :, :, cols] = piece.reshape(n2, n1, ROWS, 512).astype(jnp.bfloat16)

    rs_sends, (rs_order, _) = scatter_order()

    def landing(m):
        i2, i1, n = subs_of(m.part, m.stage)[m.sub]
        return lands[m.part][m.stage].at[0 if m.sign == 1 else 1, m.dist - 1, i2, pl.ds(i1, n)]

    scatters = {}
    for key, (m, _, _) in rs_sends.items():
        scatters[key] = remote(
            view(m, m.dist * m.sign, True), landing(m),
            rs_send.at[index[key]], rs_recv.at[index[key]], near[m.link],
        )
    for kind, what in rs_order:
        if kind == "send":
            scatters[what].start()
        elif kind == "job" and what[0] == "hid":
            hidden_rows(what[1])
        elif kind == "job":
            down(what[1], what[2])
        else:
            m = rs_sends[what][0]
            scatters[what].wait_recv()
            target = view(m, (m.dist - 1) * m.sign, True)
            target[...] = target[...] + landing(m)[...]
    for p in range(3):
        out_ref[:, p * WIDE : (p + 1) * WIDE] = toks[p][0, 0, 0, :, 0:WIDE]
    for copy in scatters.values():
        copy.wait_send()


def local(
    tokens, gate_up_weight, down_weight, expert_ids, slot_ids, gate_values, old_place, new_place
):
    count = len(messages())
    bf16, f32 = jnp.bfloat16, jnp.float32
    any_space = pl.BlockSpec(memory_space=pl.ANY)
    vmem = pl.BlockSpec(memory_space=pltpu.VMEM)
    lands = []
    for part in range(3):
        for stage in (2, 1, 0):
            n1, n2, _ = (RING[axis] for axis in ORDER[part])
            ring = RING[ORDER[part][stage]]
            shape = (n2 if stage == 2 else 1, n1 if stage else 1)
            lands.append(pltpu.VMEM((2, ring // 2, *shape, ROWS, WIDE), bf16))
    return pl.pallas_call(
        kernel,
        out_shape=jax.ShapeDtypeStruct((ROWS, 3 * WIDE), bf16),
        in_specs=[any_space] * 7,
        out_specs=vmem,
        scratch_shapes=[
            pltpu.VMEM((8, 4, 4, ROWS, WIDE + EXTRA), bf16),
            pltpu.VMEM((4, 4, 8, ROWS, WIDE), bf16),
            pltpu.VMEM((4, 4, 8, ROWS, WIDE), bf16),
            pltpu.VMEM((2, 2, SLOTS, SLIVER, 3 * WIDE), bf16),
            pltpu.VMEM((2, SLOTS, SLIVER, 3 * WIDE), bf16),
            pltpu.VMEM((8, 4, 4, ROWS, 2 * UNITS), f32),
            pltpu.VMEM((8, 4, 4, ROWS, UNITS), f32),
            pltpu.VMEM((EXTRA, UNITS), bf16),
            pltpu.VMEM((256, UNITS), bf16),
            *lands,
            pltpu.VMEM((2, ROWS), jnp.int32),
            pltpu.VMEM((2, ROWS), f32),
            pltpu.SMEM((SLOTS,), jnp.int32),
            pltpu.SMEM((SLOTS,), jnp.int32),
            pltpu.SemaphoreType.DMA((4,)),
            pltpu.SemaphoreType.DMA((6,)),
            pltpu.SemaphoreType.DMA((3,)),
            pltpu.SemaphoreType.DMA((3,)),
            pltpu.SemaphoreType.DMA((count,)),
            pltpu.SemaphoreType.DMA((count,)),
            pltpu.SemaphoreType.DMA((count,)),
            pltpu.SemaphoreType.DMA((count,)),
        ],
        compiler_params=pltpu.CompilerParams(
            collective_id=0, has_side_effects=True, vmem_limit_bytes=67043328
        ),
        name="expert_layer",
    )(tokens, gate_up_weight, down_weight, expert_ids.T, gate_values.T, old_place, new_place)


def solution(mesh):
    in_specs = (
        P(AXES, None),
        P(None, None, AXES, None),
        P(None, AXES, None),
        P(AXES, None),
        P(AXES, None),
        P(AXES, None),
        P(),
        P(),
    )
    out_specs = P(AXES, None)
    return jax.shard_map(local, mesh=mesh, in_specs=in_specs, out_specs=out_specs, check_vma=False)
```

```python
import functools
import heapq

import jax
import jax.numpy as jnp
from jax import lax
from jax.experimental import pallas as pl
from jax.experimental.pallas import tpu as pltpu
from jax.sharding import PartitionSpec as P

AXES = ("dp", "expert", "shard")
ROWS = 8
WIDE = 2048
EXTRA = 128
SLOTS = 8
SLIVER = 32
UNITS = 2 * SLOTS * SLIVER
RING = {"x": 4, "y": 4, "z": 8}
ORDER = (("x", "y", "z"), ("z", "y", "x"), ("z", "x", "y"))
RATE, LATENCY = 45500.0, 1.7
AHEAD = 3.0
GATHER_BONUS = {
    (0, 2, 1): 8.4, (2, 2, 1): -1.3, (1, 0, 1): 3.2, (2, 2, "i2", 0): 9.8, (2, 2, 2): -5.4,
    (0, 2, "i2", 3): 7.1, (2, 2, "i2", 3): 3.1, (2, 1, 1): 1.3, (2, 2, "i2", 2): -0.2, (0, 1, 1): 9.9,
    (1, 0, 3): 10.5, (1, 2, "i2", 0): -2.1, (2, 0): 13.6, (0, 2, 4): 2.1, (1, 1): 12.0,
    (0, 2, "i2", 0): -1.6, (0, 2, 2): 12.4, (1, 2, "i2", 1): -0.8, (0, 0, 2): 13.3, (1, 2, 1): 1.1,
    (1, 2, "i2", 2): -3.7, (1, 2, "i2", 3): -11.9, (0, 2, "i2", 1): 3.8, (0, 2): 9.5, (2, 0, 3): 13.3,
    (1, 2): -12.6, (1, 1, 1): 2.7, (1, 2, 2): -9.8, (1, 0, 4): -6.2, (0, 1, 2): -0.8,
    (1, 0, 2): -10.9, (2, 0, 4): -9.6, (2, 2, "i2", 1): 0.4, (1, 0): 0.1, (0, 2, "i2", 2): 12.3,
    (0, 1): 6.0, (2, 2): -7.3, (2, 1): 11.6,
}
SCATTER_BONUS = {
    (2, 2): -11.4, (0, 1): -5.1, (1, 0, 3): -1.7, (1, 0, 1): 6.8, (2, 2, "i2", 3): 7.5,
    (0, 2, 2): -3.0, (2, 1): -1.0, (1, 2, "i2", 2): -1.4, (1, 2): -0.9, (1, 0, 4): 2.1,
    (0, 1, 2): -1.5, (2, 2, 1): 3.3, (1, 1, 2): -10.2, (0, 2, 1): 3.3, (0, 2, "i2", 1): 8.6,
    (1, 2, "i2", 0): -2.1, (2, 2, "i2", 2): -0.3, (1, 1, 1): -0.2, (2, 0, 2): 0.7, (2, 0, 4): -6.7,
    (2, 0, 3): -6.4, (2, 0, 1): -9.0, (0, 0, 1): 2.7, (1, 2, "i2", 3): 1.5, (2, 0): 11.5,
    (0, 2, 4): -7.1, (0, 0): -12.4, (0, 2, 3): -0.7,
}


class Message:
    def __init__(self, part, stage, dist, sign, sub):
        self.part, self.stage, self.dist, self.sign, self.sub = part, stage, dist, sign, sub
        self.key = (part, stage, dist, sign, sub)
        self.axis = ORDER[part][stage]
        self.link = (self.axis, sign)


def position(ring_index, size):
    r = ring_index % size
    return 0 if r == 0 else (2 * r - 1 if r <= size // 2 else 2 * (size - r))


def groups(n1):
    return [(0, 1), (1, 2), (3, 1)] if n1 == 4 else [(0, 1), (1, 2), (3, 2), (5, 3)]


def subs_of(part, stage):
    n1, n2 = RING[ORDER[part][0]], RING[ORDER[part][1]]
    if stage == 0:
        return [(0, 0, 1)]
    first = [(0, i1, n) for i1, n in groups(n1)]
    if stage == 1:
        return first
    rest = [(0, 4)] if n1 == 4 else [(0, 3), (3, 5)]
    return first + [(i2, i1, n) for i2 in range(1, n2) for i1, n in rest]


def far_sign(part, stage, sub):
    subs = subs_of(part, stage)
    if stage == 0:
        return -1 if part == 2 else 1
    if stage == 1:
        return 1 if sub in (0, len(subs) - 1) else -1
    return 1 if subs[sub][0] in (0, 3) else -1


def messages():
    out = []
    for part in range(3):
        for stage in range(3):
            size = RING[ORDER[part][stage]]
            for dist in range(1, size // 2 + 1):
                for sign in (1, -1):
                    for sub in range(len(subs_of(part, stage))):
                        if dist < size // 2 or far_sign(part, stage, sub) == sign:
                            out.append(Message(part, stage, dist, sign, sub))
    return out


def blocks_of(msg, ring_index):
    i2, i1, n = subs_of(msg.part, msg.stage)[msg.sub]
    p = position(ring_index, RING[msg.axis])
    if msg.stage == 0:
        return [(0, 0, p)]
    if msg.stage == 1:
        return [(0, p, i1 + j) for j in range(n)]
    return [(p, i2, i1 + j) for j in range(n)]


def simulate(sends, recv_needs, jobs, recv_cost, timers=(), ahead=AHEAD, bonus=None):
    readers = {}
    for key, (_, _, needs) in sends.items():
        for token in needs:
            readers.setdefault(token, []).append(key)
    tails = {}

    def tail(key):
        if key not in tails:
            after = max((tail(k) for k in readers.get(("recv",) + key, [])), default=0.0)
            tails[key] = sends[key][1] / RATE + LATENCY + after
        return tails[key]

    number = {key: i for i, key in enumerate(sends)}
    missing = {key: len(needs) for key, (_, _, needs) in sends.items()}
    queues, link_free, arrivals = {}, {}, []
    done, order, ready = set(), [], []
    now = 0.0

    def offer(key):
        part, stage, dist, _, sub = key
        extra = bonus or {}
        i2 = subs_of(part, stage)[sub][0]
        rank = tail(key) + sum(extra.get(k, 0.0) for k in ((part, stage), (part, stage, dist), (part, stage, "i2", i2)))
        heapq.heappush(queues.setdefault(sends[key][0].link, []), (-rank, number[key], key))

    def finish(token):
        done.add(token)
        for key in readers.get(token, []):
            missing[key] -= 1
            if not missing[key]:
                offer(key)

    def issue():
        for link, queue in queues.items():
            while queue and link_free.get(link, 0.0) - now < ahead:
                key = heapq.heappop(queue)[2]
                order.append(("send", key))
                sent = max(now, link_free.get(link, 0.0)) + sends[key][1] / RATE
                link_free[link] = sent
                heapq.heappush(arrivals, (sent + LATENCY, key))

    for key, count in missing.items():
        if not count:
            offer(key)
    jobs, timers = list(jobs), list(timers)
    handled = 0
    issue()
    while handled < len(sends) or jobs:
        while timers and timers[0][0] <= now:
            token = timers.pop(0)[1]
            order.append(("job", token))
            finish(token)
        while arrivals and arrivals[0][0] <= now:
            ready.append(heapq.heappop(arrivals))
        pick = next((r for r in ready if recv_needs[r[1]] <= done), None)
        job = next((j for j in jobs if j[2] <= done), None)
        if pick is not None:
            ready.remove(pick)
            now += recv_cost(sends[pick[1]])
            order.append(("recv", pick[1]))
            finish(("recv",) + pick[1])
            handled += 1
        elif job is not None:
            jobs.remove(job)
            now += job[1]
            order.append(("job", job[0]))
            finish(job[0])
        else:
            times = [a[0] for a in arrivals[:1]] + [t[0] for t in timers[:1]]
            times += [free - ahead + 0.01 for link, free in link_free.items() if queues.get(link)]
            now = max(now, min(times))
        issue()
    return order, now


def gather_order():
    msgs = messages()
    source = {}
    for m in msgs:
        for b in blocks_of(m, -m.dist * m.sign):
            source[(m.part,) + b] = ("recv",) + m.key
    sends = {}
    for m in msgs:
        src = blocks_of(m, -(m.dist - 1) * m.sign)
        needs = {source[(m.part,) + b] for b in src if (m.part,) + b in source}
        width = WIDE + (EXTRA if m.part == 0 else 0)
        sends[m.key] = (m, len(src) * ROWS * width * 2, needs)
    jobs = []
    for part, slabs, i2s, held in GATE_UP_JOBS:
        needs = {v for k, v in source.items() if k[0] == part and k[1] in slabs and k[2] in i2s}
        rows = (32 if part == 0 else 64) * len(i2s) * len(slabs)
        cost = PREPARE_COST * rows + UP_COST[rows] * len(held)
        jobs.append((("up", part, slabs, i2s, held), cost, needs | {("weights", held[-1])}))
    timers = [(OWN_AT, ("weights", 0)), (PARTNER_AT, ("weights", 1))]
    return sends, simulate(sends, {m.key: set() for m in msgs}, jobs, lambda s: 0.05, timers, bonus=GATHER_BONUS)


OWN_AT, PARTNER_AT = 5.0, 20.0
PREPARE_COST = 0.0001
UP_COST = {64: 0.65, 128: 0.67, 192: 0.7, 256: 0.76, 384: 1.08}
HIDDEN_COST = (0.8, 0.4, 0.7, 1.5)
ALL = (0, 1, 2, 3)
GATE_UP_JOBS = (
    (2, (1,), ALL, (0, 1)),
    (1, (0,), ALL, (0, 1)),
    (2, (3,), (0,), (0, 1)),
    (0, (3, 4), ALL, (0, 1)),
    (2, (3,), (1, 2, 3), (0, 1)),
    (0, (7,), ALL, (0, 1)),
    (2, (0,), ALL, (0, 1)),
    (1, (1,), ALL, (0, 1)),
    (0, (5, 6), ALL, (0, 1)),
    (2, (2,), ALL, (0, 1)),
    (0, (0, 1, 2), ALL, (0, 1)),
    (1, (2,), ALL, (0, 1)),
    (1, (3,), ALL, (0, 1)),
)
DOWN_JOBS = (
    ("hid", 0), (2, (3,)), ("hid", 1), (0, (7,)), ("hid", 2), (1, (3,)),
    ("hid", 3), (0, (5, 6)), (1, (1,)), (2, (1,)), (2, (2,)), (0, (3, 4)),
    (1, (2,)), (2, (0,)), (0, (1, 2)), (1, (0,)), (0, (0,)),
)


def scatter_order():
    msgs = messages()[::-1]
    job_of = {}
    for part, slabs in DOWN_JOBS:
        if part != "hid":
            for i3 in slabs:
                job_of[(part, i3)] = ("down", part, slabs)
    adds = {}
    for m in msgs:
        for b in blocks_of(m, (m.dist - 1) * m.sign):
            adds.setdefault((m.part,) + b, []).append(m)
    sends, recv_needs = {}, {}
    for m in msgs:
        src = blocks_of(m, m.dist * m.sign)
        needs = set()
        for b in src:
            needs.add(job_of[(m.part, b[0])])
            for a in adds.get((m.part,) + b, []):
                if a.stage > m.stage or (a.stage == m.stage and a.sign == m.sign and a.dist == m.dist + 1):
                    needs.add(("recv",) + a.key)
        sends[m.key] = (m, len(src) * ROWS * WIDE * 2, needs)
        recv_needs[m.key] = {job_of[(m.part, b[0])] for b in blocks_of(m, (m.dist - 1) * m.sign)}
    jobs = []
    for part, slabs in DOWN_JOBS:
        if part == "hid":
            jobs.append((("hid", slabs), HIDDEN_COST[slabs], set()))
        else:
            jobs.append((("down", part, slabs), 0.75 * len(slabs) if part == 0 else 1.1, set()))
    return sends, simulate(sends, recv_needs, jobs, lambda s: 0.04 + s[1] * 0.8e-6, bonus=SCATTER_BONUS)


def device_at(x, y, z, core):
    x, y, z = lax.rem(x + 4, 4), lax.rem(y + 4, 4), lax.rem(z + 8, 8)
    return (lax.rem(x, 2), z, (x // 2) * 8 + y * 2 + core)


def kernel(
    tok_ref, gu_ref, dn_ref, ids_hbm, gv_hbm, old_hbm, new_hbm, out_ref,
    tok0, tok1, tok2, w_gu, w_dn, acc, scale, spread, hs,
    l30, l20, l10, l31, l21, l11, l32, l22, l12,
    ids_ref, gv_ref, old_ref, new_ref, table_sem, own_sem, w_send, w_recv, ag_send, ag_recv, rs_send, rs_recv,
):
    toks = (tok0, tok1, tok2)
    lands = ((l10, l20, l30), (l11, l21, l31), (l12, l22, l32))
    dp, z, shard = (lax.axis_index(a) for a in AXES)
    core, y, x = lax.rem(shard, 2), lax.rem(shard // 2, 4), (shard // 8) * 2 + dp
    partner = device_at(x, y, z, 1 - core)
    near = {
        ("x", 1): device_at(x + 1, y, z, core), ("x", -1): device_at(x - 1, y, z, core),
        ("y", 1): device_at(x, y + 1, z, core), ("y", -1): device_at(x, y - 1, z, core),
        ("z", 1): device_at(x, y, z + 1, core), ("z", -1): device_at(x, y, z - 1, core),
    }
    mesh_id = pl.DeviceIdType.MESH
    barrier = pltpu.get_barrier_semaphore()
    for dev in (partner, *near.values()):
        pl.semaphore_signal(barrier, inc=1, device_id=dev, device_id_type=mesh_id)

    tables = [
        pltpu.make_async_copy(src, dst, table_sem.at[i])
        for i, (src, dst) in enumerate(((ids_hbm, ids_ref), (gv_hbm, gv_ref), (old_hbm, old_ref), (new_hbm, new_ref)))
    ]
    for copy in tables:
        copy.start()
    own = [
        pltpu.make_async_copy(tok_ref.at[:, pl.ds(p * WIDE, WIDE)], toks[p].at[0, 0, 0, :, pl.ds(0, WIDE)], own_sem.at[p])
        for p in range(3)
    ]
    for copy in own:
        copy.start()
    own_w = [
        pltpu.make_async_copy(gu_ref.at[:, 0], w_gu.at[0, 0], own_sem.at[3]),
        pltpu.make_async_copy(gu_ref.at[:, 1], w_gu.at[0, 1], own_sem.at[4]),
        pltpu.make_async_copy(dn_ref, w_dn.at[0], own_sem.at[5]),
    ]
    for copy in own_w:
        copy.start()

    for copy in tables:
        copy.wait()

    lane = lax.broadcasted_iota(jnp.int32, (ROWS, EXTRA), 1)
    slot = lax.rem(lane, SLOTS)
    diagonal = lax.broadcasted_iota(jnp.int32, (ROWS, ROWS), 0) == lax.broadcasted_iota(jnp.int32, (ROWS, ROWS), 1)

    def column(ref, k):
        row = jnp.broadcast_to(ref[k : k + 1, :], (ROWS, ROWS))
        return jnp.sum(jnp.where(diagonal, row, jnp.zeros_like(row)), axis=1, keepdims=True)

    held = jnp.zeros((ROWS, EXTRA), jnp.int32)
    for j in range(SLOTS):
        held = jnp.where(slot == j, old_ref[j], held)
    weight = jnp.zeros((ROWS, EXTRA), jnp.float32)
    for k in range(2):
        ids = jnp.broadcast_to(column(ids_ref, k), (ROWS, EXTRA))
        gate = jnp.broadcast_to(column(gv_ref, k), (ROWS, EXTRA))
        place = jnp.zeros((ROWS, EXTRA), jnp.int32)
        for e in range(SLOTS):
            place = jnp.where(ids == e, new_ref[e], place)
        weight = weight + jnp.where(place == held, gate, 0.0)
    high = weight.astype(jnp.bfloat16).astype(jnp.float32)
    coded = jnp.where(lane < SLOTS, high, jnp.where(lane < 2 * SLOTS, weight - high, 0.0))
    tok0[0, 0, 0, :, WIDE:] = coded.astype(jnp.bfloat16)

    own[0].wait()
    pl.semaphore_wait(barrier, 7)

    def remote(src, dst, send, recv, dev):
        return pltpu.make_async_remote_copy(
            src_ref=src, dst_ref=dst, send_sem=send, recv_sem=recv, device_id=dev, device_id_type=mesh_id
        )

    def view(msg, ring_index, narrow):
        i3, i2, i1 = blocks_of(msg, ring_index)[0]
        n = subs_of(msg.part, msg.stage)[msg.sub][2]
        ref = toks[msg.part]
        if narrow and msg.part == 0:
            return ref.at[i3, i2, pl.ds(i1, n), :, pl.ds(0, WIDE)]
        return ref.at[i3, i2, pl.ds(i1, n)]

    ag_sends, (ag_order, _) = gather_order()
    index = {key: i for i, key in enumerate(ag_sends)}
    gathers = {}
    for key, (m, _, _) in ag_sends.items():
        source, target = view(m, -(m.dist - 1) * m.sign, False), view(m, -m.dist * m.sign, False)
        if m.part and blocks_of(m, -(m.dist - 1) * m.sign) == [(0, 0, 0)]:
            source, target = tok_ref.at[:, pl.ds(m.part * WIDE, WIDE)], target.at[0]
        gathers[key] = remote(
            source, target,
            ag_send.at[index[key]], ag_recv.at[index[key]], near[m.link],
        )
    crossing = [
        remote(gu_ref.at[:, 0], w_gu.at[1, 0], w_send.at[0], w_recv.at[0], partner),
        remote(gu_ref.at[:, 1], w_gu.at[1, 1], w_send.at[1], w_recv.at[1], partner),
        remote(dn_ref, w_dn.at[1], w_send.at[2], w_recv.at[2], partner),
    ]

    def gate_up(part, slabs, i2s, held):
        ref = toks[part]
        count = len(i2s)
        total = len(slabs) * count * ref.shape[2] * ROWS

        @pl.loop(held[0], held[-1] + 1)
        def _(group):
            right = w_gu[group, :, :, :, pl.ds(part * WIDE, WIDE)].reshape(UNITS, WIDE)
            left = ref[pl.ds(slabs[0], len(slabs)), pl.ds(i2s[0], count), :, :, pl.ds(0, WIDE)].reshape(total, WIDE)
            prod = lax.dot_general(
                left, right, (((1,), (1,)), ((), ())), preferred_element_type=jnp.float32
            )
            cols = pl.ds(pl.multiple_of(group * UNITS, UNITS), UNITS)
            if part == 0:
                for j, i3 in enumerate(slabs):
                    acc[i3, :, :, :, cols] += prod[j * 128 : (j + 1) * 128].reshape(4, 4, ROWS, UNITS)
            else:
                for i2 in range(count):
                    where = (i2s[i2], slabs[0]) if part == 1 else (slabs[0], i2s[i2])
                    acc[:, where[0], where[1], :, cols] += prod[i2 * 64 : (i2 + 1) * 64].reshape(8, ROWS, UNITS)

        if part == 0 and held[-1] == 1:
            for i3 in slabs:
                code = tok0[i3, :, :, :, pl.ds(WIDE, EXTRA)].astype(jnp.float32).reshape(128, EXTRA)
                wide = jnp.dot(code.astype(jnp.bfloat16), spread[...], preferred_element_type=jnp.float32)
                scale[i3] = wide.reshape(4, 4, ROWS, UNITS)

    crossed = False
    for kind, what in ag_order:
        if kind != "send" and not crossed:
            crossed = True
            for copy in crossing:
                copy.start()
            acc[...] = jnp.zeros_like(acc)
            code_row = lax.broadcasted_iota(jnp.int32, (EXTRA, UNITS), 0)
            unit_slot = lax.rem(lax.broadcasted_iota(jnp.int32, (EXTRA, UNITS), 1) // SLIVER, SLOTS)
            chosen = (code_row < 2 * SLOTS) & (lax.rem(code_row, SLOTS) == unit_slot)
            spread[...] = jnp.where(chosen, 1.0, 0.0).astype(jnp.bfloat16)
        if kind == "send":
            gathers[what].start()
        elif kind == "recv":
            gathers[what].wait_recv()
        elif what == ("weights", 1):
            for copy in crossing:
                copy.wait()
        elif what == ("weights", 0):
            for copy in own[1:] + own_w:
                copy.wait()
        else:
            gate_up(*what[1:])
    for copy in gathers.values():
        copy.wait_send()

    def hidden(where):
        width = UNITS // 2
        values = []
        for group in range(2):
            gate = acc[(*where, slice(None), pl.ds(group * UNITS, width))]
            up = acc[(*where, slice(None), pl.ds(group * UNITS + width, width))]
            share = scale[(*where, slice(None), pl.ds(group * width, width))]
            values.append(gate / (1.0 + jnp.exp(-gate)) * up * share)
        for group in range(2):
            acc[(*where, slice(None), pl.ds(group * width, width))] = values[group]

    def hidden_rows(step):
        if step == 0:
            pl.loop(0, 8)(lambda i: hidden((i, 3, slice(None))))
        elif step == 1:
            pl.loop(0, 3)(lambda i: hidden((7, i, slice(None))))
        elif step == 2:
            pl.loop(0, 7)(lambda i: hidden((i, pl.ds(0, 3), 3)))
        else:
            pl.loop(0, 21)(lambda i: hidden((i // 3, lax.rem(i, 3), pl.ds(0, 3))))

    def down(part, slabs):
        total = 128 * len(slabs) if part == 0 else 256
        if part == 0:
            for j, i3 in enumerate(slabs):
                hs[j * 128 : (j + 1) * 128, :] = acc[i3, :, :, :, pl.ds(0, UNITS)].reshape(128, UNITS).astype(jnp.bfloat16)
        else:
            for i2 in range(4):
                where = (i2, slabs[0]) if part == 1 else (slabs[0], i2)
                rows = acc[:, where[0], where[1], :, pl.ds(0, UNITS)].reshape(64, UNITS)
                hs[i2 * 64 : (i2 + 1) * 64, :] = rows.astype(jnp.bfloat16)

        @pl.loop(0, WIDE // 512)
        def _(n):
            cols = pl.ds(pl.multiple_of(part * WIDE + n * 512, 512), 512)
            right = w_dn[:, :, :, cols].reshape(UNITS, 512)
            prod = jnp.dot(hs[0:total, :], right, preferred_element_type=jnp.float32)
            cols = pl.ds(pl.multiple_of(n * 512, 512), 512)
            ref = toks[part]
            n2, n1 = ref.shape[1], ref.shape[2]
            for j, i3 in enumerate(slabs):
                piece = prod[j * 128 : (j + 1) * 128] if part == 0 else prod
                ref[i3, :, :, :, cols] = piece.reshape(n2, n1, ROWS, 512).astype(jnp.bfloat16)

    rs_sends, (rs_order, _) = scatter_order()

    def landing(m):
        i2, i1, n = subs_of(m.part, m.stage)[m.sub]
        return lands[m.part][m.stage].at[0 if m.sign == 1 else 1, m.dist - 1, i2, pl.ds(i1, n)]

    scatters = {}
    for key, (m, _, _) in rs_sends.items():
        scatters[key] = remote(
            view(m, m.dist * m.sign, True), landing(m),
            rs_send.at[index[key]], rs_recv.at[index[key]], near[m.link],
        )
    results = [
        pltpu.make_async_copy(toks[p].at[0, 0, 0, :, pl.ds(0, WIDE)], out_ref.at[:, pl.ds(p * WIDE, WIDE)], own_sem.at[p])
        for p in range(3)
    ]
    left = [sum(key[0] == p for key in rs_sends) for p in range(3)]
    for kind, what in rs_order:
        if kind == "send":
            scatters[what].start()
        elif kind == "job" and what[0] == "hid":
            hidden_rows(what[1])
        elif kind == "job":
            down(what[1], what[2])
        else:
            m = rs_sends[what][0]
            scatters[what].wait_recv()
            target = view(m, (m.dist - 1) * m.sign, True)
            target[...] = target[...] + landing(m)[...]
            left[m.part] -= 1
            if not left[m.part]:
                results[m.part].start()
    for copy in results:
        copy.wait()
    for copy in scatters.values():
        copy.wait_send()


def local(
    tokens, gate_up_weight, down_weight, expert_ids, slot_ids, gate_values, old_place, new_place
):
    count = len(messages())
    bf16, f32 = jnp.bfloat16, jnp.float32
    any_space = pl.BlockSpec(memory_space=pl.ANY)
    lands = []
    for part in range(3):
        for stage in (2, 1, 0):
            n1, n2, _ = (RING[axis] for axis in ORDER[part])
            ring = RING[ORDER[part][stage]]
            shape = (n2 if stage == 2 else 1, n1 if stage else 1)
            lands.append(pltpu.VMEM((2, ring // 2, *shape, ROWS, WIDE), bf16))
    return pl.pallas_call(
        kernel,
        out_shape=jax.ShapeDtypeStruct((ROWS, 3 * WIDE), bf16),
        in_specs=[any_space] * 7,
        out_specs=any_space,
        scratch_shapes=[
            pltpu.VMEM((8, 4, 4, ROWS, WIDE + EXTRA), bf16),
            pltpu.VMEM((4, 4, 8, ROWS, WIDE), bf16),
            pltpu.VMEM((4, 4, 8, ROWS, WIDE), bf16),
            pltpu.VMEM((2, 2, SLOTS, SLIVER, 3 * WIDE), bf16),
            pltpu.VMEM((2, SLOTS, SLIVER, 3 * WIDE), bf16),
            pltpu.VMEM((8, 4, 4, ROWS, 2 * UNITS), f32),
            pltpu.VMEM((8, 4, 4, ROWS, UNITS), f32),
            pltpu.VMEM((EXTRA, UNITS), bf16),
            pltpu.VMEM((256, UNITS), bf16),
            *lands,
            pltpu.VMEM((2, ROWS), jnp.int32),
            pltpu.VMEM((2, ROWS), f32),
            pltpu.SMEM((SLOTS,), jnp.int32),
            pltpu.SMEM((SLOTS,), jnp.int32),
            pltpu.SemaphoreType.DMA((4,)),
            pltpu.SemaphoreType.DMA((6,)),
            pltpu.SemaphoreType.DMA((3,)),
            pltpu.SemaphoreType.DMA((3,)),
            pltpu.SemaphoreType.DMA((count,)),
            pltpu.SemaphoreType.DMA((count,)),
            pltpu.SemaphoreType.DMA((count,)),
            pltpu.SemaphoreType.DMA((count,)),
        ],
        compiler_params=pltpu.CompilerParams(
            collective_id=0, has_side_effects=True, vmem_limit_bytes=67043328
        ),
        name="expert_layer",
    )(tokens, gate_up_weight, down_weight, expert_ids.T, gate_values.T, old_place, new_place)


def solution(mesh):
    in_specs = (
        P(AXES, None),
        P(None, None, AXES, None),
        P(None, AXES, None),
        P(AXES, None),
        P(AXES, None),
        P(AXES, None),
        P(),
        P(),
    )
    out_specs = P(AXES, None)
    return jax.shard_map(local, mesh=mesh, in_specs=in_specs, out_specs=out_specs, check_vma=False)
```
